32 devices in a mesh: row: 16 (over z, x, core), col: 2 (over y).
Axes of the slice: x: 2, y: 2, z: 4, core: 2. Of those that a mesh axis runs over, the one named last changes fastest.
Arguments:
- polar_rays: bfloat16 [32, 360, 256], P(('row', 'col')), may hold values from -6 to 6
- first_line: int32 [32, 16, 2], P('row', None, 'col'), may hold values from 0 to 359
- second_line: int32 [32, 16, 2], P('row', None, 'col'), may hold values from 0 to 179
- start_frame: float32 [3, 3, 32], P(None, None, ('row', 'col')), may hold values from -6 to 6
Outputs:
- line_scores: float32 [32, 16, 2], P('row', None, 'col')
- estimates: float32 [3, 3, 32], P(None, None, ('row', 'col'))
The draws below stay inside these ranges and needn't reach their ends.
All inputs are finite; a program needn't handle non-finite values. Where the reference program divides by a largest or mean magnitude, that divisor is 1e-20 or more.
Results may differ from the reference program's by a relative error of at most 0.0003.
Values may be sent and summed in bfloat16 or wider, within the bound.
No kernel may reach another device: no remote copies, remote signals or barrier semaphores. Data moves between devices by JAX's collectives and lax.ppermute only.
A program may use at most 64 MiB of HBM per device.

```python
import math
import jax
import jax.numpy as jnp
from jax import lax

L = 360
R = 128
ITERS = 3
N = 32
IMG_R = 2
N_ROW = 16


def set_ends(drawn, key, least, high):
    place = [jax.random.randint(jax.random.fold_in(key, axis), (), 0, length) for axis, length in enumerate(drawn.shape)]
    longest = drawn.shape.index(max(drawn.shape))
    neighbour = place[:longest] + [(place[longest] + 1) % drawn.shape[longest]] + place[longest + 1:]
    return drawn.at[tuple(place)].set(least).at[tuple(neighbour)].set(high)


def levels(stream_key, dims, pieces, smallest, largest):
    loudness = 1.0
    for axis_at, blocks in pieces:
        steps = jax.random.uniform(jax.random.fold_in(jax.random.fold_in(stream_key, 6), axis_at), (blocks,), jnp.float32, smallest / len(pieces), largest / len(pieces))
        loudness = loudness * jnp.repeat(jnp.exp(steps), dims[axis_at] // blocks).reshape((-1,) + (1,) * (len(dims) - 1 - axis_at))
    return loudness


def noise(key, dims, scale, limit, cuts=(), held_as=jnp.bfloat16):
    drawn = jax.random.normal(key, dims, jnp.float32) * scale
    if len(cuts) > 0:
        drawn = levels(key, dims, cuts, -0.22, 0.18) * drawn
    return jnp.clip(drawn, min=-limit, max=limit).astype(held_as)


def setup_inputs(seed: int = 0) -> dict:
    seeds = jax.random.split(jax.random.key(seed), 5)
    return {
        "polar_rays": noise(seeds[0], (N, L, 2 * R), 1.0, 6.0, ((0, 32),)),
        "first_line": set_ends(jax.random.randint(seeds[1], (N, N_ROW, IMG_R), 0, L), jax.random.fold_in(seeds[1], 1), 0, L - 1).astype(jnp.int32),
        "second_line": set_ends(jax.random.randint(seeds[2], (N, N_ROW, IMG_R), 0, L // 2), jax.random.fold_in(seeds[2], 1), 0, (L // 2) - 1).astype(jnp.int32),
        "start_frame": noise(seeds[3], (3, 3, N), 1.0, 6.0, ((2, 32),), jnp.float32),
    }


def unit_vectors(angle):
    phases = angle.astype(jnp.float32) * (2.0 * math.pi / L)
    return jnp.stack([jnp.cos(phases), jnp.sin(phases), jnp.ones_like(phases)])

def lower_solve(factor, values):
    first_row = values[0] / factor[0, 0]
    second_row = (values[1] - factor[1, 0] * first_row) / factor[1, 1]
    third_row = (values[2] - factor[2, 0] * first_row - factor[2, 1] * second_row) / factor[2, 2]
    return jnp.stack([first_row, second_row, third_row])

def reference(polar_rays, first_line, second_line, start_frame):
    image_count = polar_rays.shape[0]
    first_table = first_line.reshape(image_count, image_count)
    second_table = second_line.reshape(image_count, image_count)
    real_rays = polar_rays.astype(jnp.float32)
    half_rays = real_rays[:, :L // 2]
    exact = lax.Precision.HIGHEST

    def score_row(inputs):
        own_rays, first_row, second_row = inputs
        corr = jnp.einsum('ar,jbr->jab', own_rays, half_rays, precision=exact)
        center = corr - lax.optimization_barrier(jnp.mean(corr, axis=(1, 2), keepdims=True))
        spread = lax.optimization_barrier(jnp.mean(jnp.abs(center), axis=(1, 2)))
        picked = jnp.take_along_axis(center, first_row[:, None, None], axis=1)[:, 0, :]
        picked = jnp.take_along_axis(picked, second_row[:, None], axis=1)[:, 0]
        return picked / (spread + 1e-05)
    scores = lax.map(score_row, (real_rays, first_table, second_table))
    first_units = unit_vectors(first_table)
    second_weighted = scores[None] * unit_vectors(second_table)
    frames = start_frame
    for turn_index in range(ITERS):
        mixed = jnp.einsum('qij,kqj->kij', second_weighted, frames, precision=exact)
        applied = jnp.einsum('pij,kij->kpi', first_units, mixed, precision=exact)
        gram_matrix = jnp.einsum('kpi,lpi->kl', applied, applied, precision=exact)
        factor = jnp.linalg.cholesky(gram_matrix)
        frames = lower_solve(factor, applied)
    return (scores.reshape(first_line.shape), jnp.sqrt(jnp.float32(image_count)) * frames)
```

```python
import functools
import math

import jax
import jax.numpy as jnp
from jax import lax
from jax.experimental import pallas as pl
from jax.experimental.pallas import tpu as pltpu
from jax.sharding import PartitionSpec as P

ITERS = 3
LANES = 128
PAIR = 2


class Plan:
    def __init__(self, rows, cols):
        self.rows, self.cols = rows, cols
        self.depth = rows // (PAIR * PAIR)
        self.count = rows * cols
        self.firsts = PAIR * cols
        self.seconds = PAIR * self.depth
        self.pairs = self.firsts * self.seconds
        self.width = -(-(3 * self.pairs + 9) // LANES) * LANES
        self.table = -(-2 * self.rows * self.cols // LANES) * LANES

    def flat(self, z, x, core, c):
        return ((z * PAIR + x) * PAIR + core) * self.cols + c


def position(plan):
    row, c = lax.axis_index("row"), lax.axis_index("col")
    return row // (PAIR * PAIR), (row // PAIR) % PAIR, row % PAIR, c


def prepare_kernel(plan, half, rays_ref, first_ref, second_ref, half_ref, table_ref, sem):
    copy = pltpu.make_async_copy(rays_ref.at[:, pl.ds(0, half)], half_ref, sem)
    copy.start()
    parts = [first_ref[c] for c in range(plan.cols)] + [second_ref[c] for c in range(plan.cols)]
    spare = plan.table - 2 * plan.rows * plan.cols
    if spare:
        parts.append(jnp.zeros((1, spare), jnp.int32))
    table_ref[...] = jnp.concatenate(parts, axis=1)
    copy.wait()


def score_kernel(plan, rays, half, *refs):
    fulls = refs[: plan.firsts]
    halves = refs[plan.firsts : plan.firsts + plan.seconds]
    own_table, next_table, start_ref, message_ref = refs[plan.firsts + plan.seconds : -6]
    full_rows, half_rows, first_rows, second_rows, parts, means = refs[-6:]
    z, x, core, c = position(plan)
    depth = fulls[0].shape[2]
    scale = 1.0 / (rays * half)

    full_sums, half_sums = [], []
    for n, ref in enumerate(fulls):
        values = ref[0].astype(jnp.float32)
        full_rows[n] = values
        full_sums.append(jnp.sum(values, axis=0, keepdims=True))
    for n, ref in enumerate(halves):
        values = ref[0, :half].astype(jnp.float32)
        half_rows[n] = values
        half_sums.append(jnp.sum(values, axis=0, keepdims=True))
    half_sum = jnp.concatenate(half_sums, axis=0)
    for n in range(plan.firsts):
        means[pl.ds(n * plan.seconds, plan.seconds), :] = jnp.broadcast_to(
            jnp.sum(half_sum * full_sums[n], axis=1, keepdims=True) * scale, (plan.seconds, LANES)
        )

    lane = lax.broadcasted_iota(jnp.int32, (1, plan.width), 1)
    lines = jnp.zeros((1, plan.width), jnp.int32)
    own_slot = (((x * plan.cols + c) * plan.depth) + z) * PAIR + core
    for n in range(plan.firsts):
        dx, dc = n // plan.cols, n % plan.cols
        table = next_table if dx else own_table
        for m in range(plan.seconds):
            dz, dk = m // PAIR, m % PAIR
            pair = n * plan.seconds + m
            at = (c ^ dc) * plan.rows + ((z ^ dz) * PAIR + x) * PAIR + (core ^ dk)
            a = table[0, at]
            b = table[0, plan.rows * plan.cols + at]
            first_rows[pl.ds(pair, 1), :] = full_rows[n, pl.ds(a, 1), :]
            second_rows[pl.ds(pair, 1), :] = half_rows[m, pl.ds(b, 1), :]
            slot = own_slot ^ pair
            lines = jnp.where(lane == plan.pairs + slot, a, lines)
            lines = jnp.where(lane == 2 * plan.pairs + slot, b, lines)
            corr = lax.dot_general(
                halves[m][0, :half], fulls[n][0], (((1,), (1,)), ((), ())), preferred_element_type=jnp.float32
            )
            center = means[pl.ds(pair, 1), 0:1]
            parts[pl.ds(pair, 1), :] = jnp.sum(jnp.abs(corr - center), axis=0, keepdims=True)

    center = means[:, 0:1]
    spread = jnp.sum(parts[...], axis=1, keepdims=True) * scale
    picked = jnp.sum(first_rows[...] * second_rows[...], axis=1, keepdims=True)
    score = (picked - center) / (spread + 1e-05)
    wide = (plan.pairs, plan.width)
    to = own_slot ^ lax.broadcasted_iota(jnp.int32, wide, 0)
    here = lax.broadcasted_iota(jnp.int32, wide, 1) == to
    message = jnp.sum(jnp.where(here, score, 0.0), axis=0, keepdims=True) + lines.astype(jnp.float32)
    for k in range(3):
        for q in range(3):
            message = jnp.where(lane == 3 * plan.pairs + 3 * k + q, start_ref[k, 0, q], message)
    message_ref[...] = jnp.broadcast_to(message[None], message_ref.shape)


def power_kernel(plan, rays, gathered_ref, scores_ref, frames_ref, rows_ref, sorted_ref, matrix_ref):
    z, x, core, c = position(plan)
    count, seconds = plan.count, plan.seconds
    for device in range(count):
        dz, rest = divmod(device, PAIR * PAIR * plan.cols)
        dx, rest = divmod(rest, PAIR * plan.cols)
        dk, dc = divmod(rest, plan.cols)
        rows_ref[pl.ds((dx * plan.cols + dc) * seconds + dz * PAIR + dk, 1), :] = gathered_ref[device]

    lane = lax.broadcasted_iota(jnp.int32, (seconds, plan.width), 1)
    block = (lane // seconds) % plan.firsts
    for to in range(plan.firsts):
        mixed = jnp.zeros((seconds, plan.width), jnp.float32)
        for b in range(plan.firsts):
            moved = rows_ref[b * seconds : (b + 1) * seconds, :]
            if b != to:
                moved = jnp.roll(moved, (b - to) * seconds, axis=1)
            mixed = jnp.where(block == b, moved, mixed)
        sorted_ref[to * seconds : (to + 1) * seconds, :] = mixed

    score = sorted_ref[:, :count]
    turn = 2.0 * math.pi / rays
    first = sorted_ref[:, count : 2 * count] * turn
    second = sorted_ref[:, 2 * count : 3 * count] * turn
    weighted = jnp.concatenate([score * jnp.cos(second), score * jnp.sin(second), score], axis=1)
    for p, unit in enumerate((jnp.cos(first), jnp.sin(first))):
        matrix_ref[p * count : (p + 1) * count, :] = weighted * jnp.concatenate([unit] * 3, axis=1)
    matrix_ref[2 * count :, :] = weighted

    begin = 3 * plan.pairs
    tile = begin // LANES * LANES
    turned = jnp.transpose(rows_ref[:, tile : tile + LANES])
    at = begin - tile
    frames = [
        jnp.concatenate([turned[at + 3 * k + q : at + 3 * k + q + 1] for q in range(3)], axis=1) for k in range(3)
    ]
    pad = jnp.zeros((5, 3 * count), jnp.float32)
    for _ in range(ITERS):
        stacked = jnp.concatenate(frames + [pad], axis=0)
        mixed = lax.dot_general(
            stacked,
            matrix_ref[...],
            (((1,), (1,)), ((), ())),
            precision=lax.Precision.HIGHEST,
            preferred_element_type=jnp.float32,
        )
        y = [mixed[k : k + 1] for k in range(3)]

        def gram(k, l):
            return jnp.sum(y[k] * y[l], axis=1, keepdims=True)

        f00 = jnp.sqrt(gram(0, 0))
        f10 = gram(1, 0) / f00
        f20 = gram(2, 0) / f00
        f11 = jnp.sqrt(gram(1, 1) - f10 * f10)
        f21 = (gram(2, 1) - f20 * f10) / f11
        f22 = jnp.sqrt(gram(2, 2) - f20 * f20 - f21 * f21)
        v0 = y[0] / f00
        v1 = (y[1] - f10 * v0) / f11
        v2 = (y[2] - f20 * v0 - f21 * v1) / f22
        frames = [v0, v1, v2]

    own = (x * plan.cols + c) * seconds + z * PAIR + core
    wide = lax.broadcasted_iota(jnp.int32, (1, 3 * count), 1)
    three = lax.broadcasted_iota(jnp.int32, (1, 3), 1)
    for k in range(3):
        out = jnp.zeros((1, 3), jnp.float32)
        for q in range(3):
            value = jnp.sum(jnp.where(wide == q * count + own, frames[k], 0.0), axis=1, keepdims=True)
            out = jnp.where(three == q, value, out)
        frames_ref[k] = math.sqrt(count) * out

    source = lax.broadcasted_iota(jnp.int32, (seconds, plan.rows), 0)
    target = lax.broadcasted_iota(jnp.int32, (seconds, plan.rows), 1)
    lines = [jnp.zeros((1, plan.rows), jnp.float32) for _ in range(plan.cols)]
    for dx in range(PAIR):
        row = rows_ref[pl.ds((dx * plan.cols + c) * seconds + z * PAIR + core, 1), :]
        spread = (target == (source // PAIR) * (PAIR * PAIR) + dx * PAIR + source % PAIR).astype(jnp.float32)
        for dc in range(plan.cols):
            low = row[:, dc * seconds : (dc + 1) * seconds]
            high = row[:, (plan.cols + dc) * seconds : (plan.cols + dc + 1) * seconds]
            part = jnp.broadcast_to(jnp.where(x == 1, high, low), (8, seconds))
            moved = lax.dot_general(
                part,
                spread,
                (((1,), (0,)), ((), ())),
                precision=lax.Precision.HIGHEST,
                preferred_element_type=jnp.float32,
            )
            lines[dc] = lines[dc] + moved[0:1]
    for dc in range(plan.cols):
        scores_ref[dc] = lines[dc]


def per_device(plan, polar_rays, first_line, second_line, start_frame):
    _, rays, depth = polar_rays.shape
    half = rays // 2
    half_tiled = -(-half // 8) * 8
    axes = ("row", "col")
    vmem = pl.BlockSpec(memory_space=pltpu.VMEM)
    smem = pl.BlockSpec(memory_space=pltpu.SMEM)
    anywhere = pl.BlockSpec(memory_space=pl.ANY)

    def swap(value, distance):
        return lax.ppermute(value, axes, [(n, n ^ distance) for n in range(plan.count)])

    first = jnp.transpose(first_line, (0, 2, 1))
    second = jnp.transpose(second_line, (0, 2, 1))
    half_rays, own_table = pl.pallas_call(
        functools.partial(prepare_kernel, plan, half_tiled),
        out_shape=(
            jax.ShapeDtypeStruct((1, half_tiled, depth), polar_rays.dtype),
            jax.ShapeDtypeStruct((1, plan.table), jnp.int32),
        ),
        in_specs=[anywhere, vmem, vmem],
        out_specs=(vmem, vmem),
        scratch_shapes=[pltpu.SemaphoreType.DMA],
        name="prepare",
    )(polar_rays, first, second)

    next_table = swap(own_table, plan.flat(0, 1, 0, 0))
    fulls = [polar_rays] + [
        swap(polar_rays, plan.flat(0, n // plan.cols, 0, n % plan.cols)) for n in range(1, plan.firsts)
    ]
    deep = [half_rays] + [swap(half_rays, plan.flat(dz, 0, 0, 0)) for dz in range(1, plan.depth)]
    halves = []
    for piece in deep:
        halves += [piece, swap(piece, plan.flat(0, 0, 1, 0))]

    message = pl.pallas_call(
        functools.partial(score_kernel, plan, rays, half),
        out_shape=jax.ShapeDtypeStruct((plan.count, 1, plan.width), jnp.float32),
        in_specs=[vmem] * (plan.firsts + plan.seconds) + [smem, smem, smem],
        out_specs=vmem,
        scratch_shapes=[
            pltpu.VMEM((plan.firsts, rays, depth), jnp.float32),
            pltpu.VMEM((plan.seconds, half, depth), jnp.float32),
            pltpu.VMEM((plan.pairs, depth), jnp.float32),
            pltpu.VMEM((plan.pairs, depth), jnp.float32),
            pltpu.VMEM((plan.pairs, rays), jnp.float32),
            pltpu.VMEM((plan.pairs, LANES), jnp.float32),
        ],
        name="score",
    )(*fulls, *halves, own_table, next_table, jnp.transpose(start_frame, (0, 2, 1)))

    gathered = lax.all_to_all(message, axes, 0, 0, tiled=True)

    scores, frames = pl.pallas_call(
        functools.partial(power_kernel, plan, rays),
        out_shape=(
            jax.ShapeDtypeStruct((plan.cols, 1, plan.rows), jnp.float32),
            jax.ShapeDtypeStruct((3, 1, 3), jnp.float32),
        ),
        in_specs=[vmem],
        out_specs=(vmem, vmem),
        scratch_shapes=[
            pltpu.VMEM((plan.count, plan.width), jnp.float32),
            pltpu.VMEM((plan.count, plan.width), jnp.float32),
            pltpu.VMEM((3 * plan.count, 3 * plan.count), jnp.float32),
        ],
        name="power",
    )(gathered)
    return jnp.transpose(scores, (0, 2, 1)), jnp.transpose(frames, (0, 2, 1))


def solution(mesh):
    plan = Plan(mesh.shape["row"], mesh.shape["col"])
    placed = (
        P(("row", "col"), None, None),
        P("row", None, "col"),
        P("row", None, "col"),
        P(None, None, ("row", "col")),
    )
    return jax.shard_map(
        functools.partial(per_device, plan),
        mesh=mesh,
        in_specs=placed,
        out_specs=(P("row", None, "col"), P(None, None, ("row", "col"))),
        check_vma=False,
    )
```

```python
import functools
import math

import jax
import jax.numpy as jnp
from jax import lax
from jax.experimental import pallas as pl
from jax.experimental.pallas import tpu as pltpu
from jax.sharding import PartitionSpec as P

ITERS = 3
LANES = 128
SCORE_VMEM = 24 << 20
POWER_VMEM = 16 << 20
PAIR = 2


class Plan:
    def __init__(self, rows, cols):
        self.rows, self.cols = rows, cols
        self.depth = rows // (PAIR * PAIR)
        self.count = rows * cols
        self.firsts = PAIR * cols
        self.seconds = PAIR * self.depth
        self.pairs = self.firsts * self.seconds
        self.width = -(-(3 * self.pairs + 9) // LANES) * LANES
        self.table = -(-2 * self.rows * self.cols // LANES) * LANES

    def flat(self, z, x, core, c):
        return ((z * PAIR + x) * PAIR + core) * self.cols + c


def position():
    row, c = lax.axis_index("row"), lax.axis_index("col")
    return row // (PAIR * PAIR), (row // PAIR) % PAIR, row % PAIR, c


def prepare_kernel(plan, half, rays_ref, first_ref, second_ref, half_ref, table_ref, sem):
    copy = pltpu.make_async_copy(rays_ref.at[:, pl.ds(0, half)], half_ref, sem)
    copy.start()
    parts = [first_ref[c] for c in range(plan.cols)] + [second_ref[c] for c in range(plan.cols)]
    spare = plan.table - 2 * plan.rows * plan.cols
    if spare:
        parts.append(jnp.zeros((1, spare), jnp.int32))
    table_ref[...] = jnp.concatenate(parts, axis=1)
    copy.wait()


def score_kernel(plan, rays, half, *refs):
    fulls = refs[: plan.firsts]
    halves = refs[plan.firsts : plan.firsts + plan.seconds]
    own_table, next_table, start_ref, message_ref = refs[plan.firsts + plan.seconds : -6]
    full_rows, half_rows, first_rows, second_rows, parts, means = refs[-6:]
    z, x, core, c = position()
    scale = 1.0 / (rays * half)

    full_sums, half_sums = [], []
    for n, ref in enumerate(fulls):
        values = ref[0].astype(jnp.float32)
        full_rows[n] = values
        full_sums.append(jnp.sum(values, axis=0, keepdims=True))
    for n, ref in enumerate(halves):
        values = ref[0, :half].astype(jnp.float32)
        half_rows[n] = values
        half_sums.append(jnp.sum(values, axis=0, keepdims=True))
    half_sum = jnp.concatenate(half_sums, axis=0)
    for n in range(plan.firsts):
        means[pl.ds(n * plan.seconds, plan.seconds), :] = jnp.broadcast_to(
            jnp.sum(half_sum * full_sums[n], axis=1, keepdims=True) * scale, (plan.seconds, LANES)
        )

    lane = lax.broadcasted_iota(jnp.int32, (1, plan.width), 1)
    lines = jnp.zeros((1, plan.width), jnp.int32)
    own_slot = (((x * plan.cols + c) * plan.depth) + z) * PAIR + core
    for n in range(plan.firsts):
        dx, dc = n // plan.cols, n % plan.cols
        table = next_table if dx else own_table
        for m in range(plan.seconds):
            dz, dk = m // PAIR, m % PAIR
            pair = n * plan.seconds + m
            at = (c ^ dc) * plan.rows + ((z ^ dz) * PAIR + x) * PAIR + (core ^ dk)
            a = table[0, at]
            b = table[0, plan.rows * plan.cols + at]
            first_rows[pl.ds(pair, 1), :] = full_rows[n, pl.ds(a, 1), :]
            second_rows[pl.ds(pair, 1), :] = half_rows[m, pl.ds(b, 1), :]
            slot = own_slot ^ pair
            lines = jnp.where(lane == plan.pairs + slot, a, lines)
            lines = jnp.where(lane == 2 * plan.pairs + slot, b, lines)
            corr = lax.dot_general(
                halves[m][0, :half], fulls[n][0], (((1,), (1,)), ((), ())), preferred_element_type=jnp.float32
            )
            center = means[pl.ds(pair, 1), 0:1]
            parts[pl.ds(pair, 1), :] = jnp.sum(jnp.abs(corr - center), axis=0, keepdims=True)

    center = means[:, 0:1]
    spread = jnp.sum(parts[...], axis=1, keepdims=True) * scale
    picked = jnp.sum(first_rows[...] * second_rows[...], axis=1, keepdims=True)
    score = (picked - center) / (spread + 1e-05)
    wide = (plan.pairs, plan.width)
    to = own_slot ^ lax.broadcasted_iota(jnp.int32, wide, 0)
    here = lax.broadcasted_iota(jnp.int32, wide, 1) == to
    message = jnp.sum(jnp.where(here, score, 0.0), axis=0, keepdims=True) + lines.astype(jnp.float32)
    for k in range(3):
        for q in range(3):
            message = jnp.where(lane == 3 * plan.pairs + 3 * k + q, start_ref[k, 0, q], message)
    message_ref[...] = jnp.broadcast_to(message[None], message_ref.shape)


def power_kernel(plan, rays, gathered_ref, scores_ref, frames_ref, rows_ref, sorted_ref, matrix_ref):
    z, x, core, c = position()
    count, seconds = plan.count, plan.seconds
    for device in range(count):
        dz, rest = divmod(device, PAIR * PAIR * plan.cols)
        dx, rest = divmod(rest, PAIR * plan.cols)
        dk, dc = divmod(rest, plan.cols)
        rows_ref[pl.ds((dx * plan.cols + dc) * seconds + dz * PAIR + dk, 1), :] = gathered_ref[device]

    lane = lax.broadcasted_iota(jnp.int32, (seconds, plan.width), 1)
    block = (lane // seconds) % plan.firsts
    for to in range(plan.firsts):
        mixed = jnp.zeros((seconds, plan.width), jnp.float32)
        for b in range(plan.firsts):
            moved = rows_ref[b * seconds : (b + 1) * seconds, :]
            if b != to:
                moved = jnp.roll(moved, (b - to) * seconds, axis=1)
            mixed = jnp.where(block == b, moved, mixed)
        sorted_ref[to * seconds : (to + 1) * seconds, :] = mixed

    score = sorted_ref[:, :count]
    turn = 2.0 * math.pi / rays
    first = sorted_ref[:, count : 2 * count] * turn
    second = sorted_ref[:, 2 * count : 3 * count] * turn
    weighted = jnp.concatenate([score * jnp.cos(second), score * jnp.sin(second), score], axis=1)
    for p, unit in enumerate((jnp.cos(first), jnp.sin(first))):
        matrix_ref[p * count : (p + 1) * count, :] = weighted * jnp.concatenate([unit] * 3, axis=1)
    matrix_ref[2 * count :, :] = weighted

    begin = 3 * plan.pairs
    tile = begin // LANES * LANES
    turned = jnp.transpose(rows_ref[:, tile : tile + LANES])
    at = begin - tile
    frames = [
        jnp.concatenate([turned[at + 3 * k + q : at + 3 * k + q + 1] for q in range(3)], axis=1) for k in range(3)
    ]
    pad = jnp.zeros((5, 3 * count), jnp.float32)
    for _ in range(ITERS):
        stacked = jnp.concatenate(frames + [pad], axis=0)
        mixed = lax.dot_general(
            stacked,
            matrix_ref[...],
            (((1,), (1,)), ((), ())),
            precision=lax.Precision.HIGHEST,
            preferred_element_type=jnp.float32,
        )
        y = [mixed[k : k + 1] for k in range(3)]

        def gram(k, l):
            return jnp.sum(y[k] * y[l], axis=1, keepdims=True)

        f00 = jnp.sqrt(gram(0, 0))
        f10 = gram(1, 0) / f00
        f20 = gram(2, 0) / f00
        f11 = jnp.sqrt(gram(1, 1) - f10 * f10)
        f21 = (gram(2, 1) - f20 * f10) / f11
        f22 = jnp.sqrt(gram(2, 2) - f20 * f20 - f21 * f21)
        v0 = y[0] / f00
        v1 = (y[1] - f10 * v0) / f11
        v2 = (y[2] - f20 * v0 - f21 * v1) / f22
        frames = [v0, v1, v2]

    own = (x * plan.cols + c) * seconds + z * PAIR + core
    wide = lax.broadcasted_iota(jnp.int32, (1, 3 * count), 1)
    three = lax.broadcasted_iota(jnp.int32, (1, 3), 1)
    for k in range(3):
        out = jnp.zeros((1, 3), jnp.float32)
        for q in range(3):
            value = jnp.sum(jnp.where(wide == q * count + own, frames[k], 0.0), axis=1, keepdims=True)
            out = jnp.where(three == q, value, out)
        frames_ref[k] = math.sqrt(count) * out

    source = lax.broadcasted_iota(jnp.int32, (seconds, plan.rows), 0)
    target = lax.broadcasted_iota(jnp.int32, (seconds, plan.rows), 1)
    lines = [jnp.zeros((1, plan.rows), jnp.float32) for _ in range(plan.cols)]
    for dx in range(PAIR):
        row = rows_ref[pl.ds((dx * plan.cols + c) * seconds + z * PAIR + core, 1), :]
        spread = (target == (source // PAIR) * (PAIR * PAIR) + dx * PAIR + source % PAIR).astype(jnp.float32)
        for dc in range(plan.cols):
            low = row[:, dc * seconds : (dc + 1) * seconds]
            high = row[:, (plan.cols + dc) * seconds : (plan.cols + dc + 1) * seconds]
            part = jnp.broadcast_to(jnp.where(x == 1, high, low), (8, seconds))
            moved = lax.dot_general(
                part,
                spread,
                (((1,), (0,)), ((), ())),
                precision=lax.Precision.HIGHEST,
                preferred_element_type=jnp.float32,
            )
            lines[dc] = lines[dc] + moved[0:1]
    for dc in range(plan.cols):
        scores_ref[dc] = lines[dc]


def scored(plan, polar_rays, first_line, second_line, start_frame):
    _, rays, depth = polar_rays.shape
    half = rays // 2
    half_tiled = -(-half // 8) * 8
    axes = ("row", "col")
    vmem = pl.BlockSpec(memory_space=pltpu.VMEM)
    smem = pl.BlockSpec(memory_space=pltpu.SMEM)
    anywhere = pl.BlockSpec(memory_space=pl.ANY)

    def swap(value, distance):
        return lax.ppermute(value, axes, [(n, n ^ distance) for n in range(plan.count)])

    first = jnp.transpose(first_line, (0, 2, 1))
    second = jnp.transpose(second_line, (0, 2, 1))
    half_rays, own_table = pl.pallas_call(
        functools.partial(prepare_kernel, plan, half_tiled),
        out_shape=(
            jax.ShapeDtypeStruct((1, half_tiled, depth), polar_rays.dtype),
            jax.ShapeDtypeStruct((1, plan.table), jnp.int32),
        ),
        in_specs=[anywhere, vmem, vmem],
        out_specs=(vmem, vmem),
        scratch_shapes=[pltpu.SemaphoreType.DMA],
        compiler_params=pltpu.CompilerParams(vmem_limit_bytes=1 << 20),
        name="prepare",
    )(polar_rays, first, second)

    next_table = swap(own_table, plan.flat(0, 1, 0, 0))
    fulls = [polar_rays] + [
        swap(polar_rays, plan.flat(0, n // plan.cols, 0, n % plan.cols)) for n in range(1, plan.firsts)
    ]
    deep = [half_rays] + [swap(half_rays, plan.flat(dz, 0, 0, 0)) for dz in range(1, plan.depth)]
    halves = []
    for piece in deep:
        halves += [piece, swap(piece, plan.flat(0, 0, 1, 0))]

    message = pl.pallas_call(
        functools.partial(score_kernel, plan, rays, half),
        out_shape=jax.ShapeDtypeStruct((plan.count, 1, plan.width), jnp.float32),
        in_specs=[vmem] * (plan.firsts + plan.seconds) + [smem, smem, smem],
        out_specs=vmem,
        compiler_params=pltpu.CompilerParams(vmem_limit_bytes=SCORE_VMEM),
        scratch_shapes=[
            pltpu.VMEM((plan.firsts, rays, depth), jnp.float32),
            pltpu.VMEM((plan.seconds, half, depth), jnp.float32),
            pltpu.VMEM((plan.pairs, depth), jnp.float32),
            pltpu.VMEM((plan.pairs, depth), jnp.float32),
            pltpu.VMEM((plan.pairs, rays), jnp.float32),
            pltpu.VMEM((plan.pairs, LANES), jnp.float32),
        ],
        name="score",
    )(*fulls, *halves, own_table, next_table, jnp.transpose(start_frame, (0, 2, 1)))

    gathered = lax.all_to_all(message, axes, 0, 0, tiled=True)

    scores, frames = pl.pallas_call(
        functools.partial(power_kernel, plan, rays),
        out_shape=(
            jax.ShapeDtypeStruct((plan.cols, 1, plan.rows), jnp.float32),
            jax.ShapeDtypeStruct((3, 1, 3), jnp.float32),
        ),
        in_specs=[vmem],
        out_specs=(vmem, vmem),
        compiler_params=pltpu.CompilerParams(vmem_limit_bytes=POWER_VMEM),
        scratch_shapes=[
            pltpu.VMEM((plan.count, plan.width), jnp.float32),
            pltpu.VMEM((plan.count, plan.width), jnp.float32),
            pltpu.VMEM((3 * plan.count, 3 * plan.count), jnp.float32),
        ],
        name="power",
    )(gathered)
    return jnp.transpose(scores, (0, 2, 1)), jnp.transpose(frames, (0, 2, 1))


def per_device(plan, *arrays):
    return scored(plan, *arrays)


def solution(mesh):
    plan = Plan(mesh.shape["row"], mesh.shape["col"])
    placed = (
        P(("row", "col"), None, None),
        P("row", None, "col"),
        P("row", None, "col"),
        P(None, None, ("row", "col")),
    )
    return jax.shard_map(
        functools.partial(per_device, plan),
        mesh=mesh,
        in_specs=placed,
        out_specs=(P("row", None, "col"), P(None, None, ("row", "col"))),
        check_vma=False,
    )
```

```python
import functools
import math

import jax
import jax.numpy as jnp
from jax import lax
from jax.experimental import pallas as pl
from jax.experimental.pallas import tpu as pltpu
from jax.sharding import PartitionSpec as P

ITERS = 3
LANES = 128
TABLE = 8
CHUNK = 256
GROUP = 8
SCORE_VMEM = 24 << 20
POWER_VMEM = 16 << 20
PAIR = 2


class Plan:
    def __init__(self, rows, cols):
        self.rows, self.cols = rows, cols
        self.depth = rows // (PAIR * PAIR)
        self.count = rows * cols
        self.firsts = PAIR * cols
        self.seconds = PAIR * self.depth
        self.pairs = self.firsts * self.seconds
        self.width = -(-(3 * self.pairs + 9) // LANES) * LANES
        self.index = -(-self.pairs // LANES) * LANES

    def flat(self, z, x, core, c):
        return ((z * PAIR + x) * PAIR + core) * self.cols + c


def position():
    row, c = lax.axis_index("row"), lax.axis_index("col")
    return row // (PAIR * PAIR), (row // PAIR) % PAIR, row % PAIR, c


def prepare_kernel(
    plan, rays_ref, first_ref, second_ref, start_ref, full_ref, half_ref, frame_ref, first_row, second_row, sems
):
    rays, depth = rays_ref.shape[1:]
    half = half_ref.shape[1]
    moves = (
        (rays_ref.at[:, pl.ds(0, half)], half_ref),
        (rays_ref.at[:, pl.ds(0, half)], full_ref.at[:, pl.ds(0, half)]),
        (rays_ref.at[:, pl.ds(half, rays - half)], full_ref.at[:, pl.ds(half, rays - half)]),
        (first_ref, first_row),
        (second_ref, second_row),
        (start_ref, frame_ref),
    )
    copies = [pltpu.make_async_copy(*move, sems.at[k]) for k, move in enumerate(moves)]
    for copy in copies:
        copy.start()
    for copy in copies:
        copy.wait()

    def row(table_ref):
        parts = [table_ref[c] for c in range(plan.cols)]
        spare = depth - plan.rows * plan.cols
        return jnp.concatenate(parts + [jnp.zeros((1, spare), jnp.int32)] * (spare > 0), axis=1)

    first, second = row(first_row), row(second_row)
    rows = jnp.concatenate([first >> 1, first & 1, second, jnp.zeros((TABLE - 3, depth), jnp.int32)], axis=0)
    full_ref[0, rays : rays + TABLE] = rows.astype(jnp.float32).astype(full_ref.dtype)


def pick_lines(own_table, next_table, own_at, next_at):
    chosen = 0.0
    for table, at in ((own_table, own_at), (next_table, next_at)):
        column = lax.broadcasted_iota(jnp.int32, (table.shape[1], at.shape[1]), 0)
        here = jnp.where(column == at, 1.0, 0.0).astype(table.dtype)
        chosen = chosen + jnp.dot(table, here, preferred_element_type=jnp.float32)
    return 2.0 * chosen[0:1] + chosen[1:2], chosen[2:3]


def lines(plan, own_table, next_table):
    z, x, core, c = position()
    number = lax.broadcasted_iota(jnp.int32, (1, plan.pairs), 1)
    dk, rest = number % PAIR, number // PAIR
    dz, rest = rest % plan.depth, rest // plan.depth
    dc, dx = rest % plan.cols, rest // plan.cols
    at = (c ^ dc) * plan.rows + ((z ^ dz) * PAIR + x) * PAIR + (core ^ dk)
    paired = pick_lines(own_table, next_table, jnp.where(dx == 0, at, -1), jnp.where(dx == 0, -1, at))
    at = dc * plan.rows + (dz * PAIR + x) * PAIR + dk
    sent = pick_lines(own_table, next_table, jnp.where(dx == x, at, -1), jnp.where(dx == x, -1, at))
    return paired, sent


def load_firsts(refs, stack, rows):
    sums = []
    for n, ref in enumerate(refs):
        stack[n, : ref.shape[1]] = ref[0]
        values = ref[0, : rows.shape[1]].astype(jnp.float32)
        rows[n] = values
        sums.append(jnp.sum(values, axis=0, keepdims=True))
    return sums


def load_seconds(refs, half, stack, rows):
    sums = []
    for m, ref in enumerate(refs):
        stack[m, : ref.shape[1]] = ref[0]
        values = ref[0, :half].astype(jnp.float32)
        rows[m] = values
        sums.append(jnp.sum(values, axis=0, keepdims=True))
    return sums


def cross(rays, half, firsts, seconds, first_sums, second_sums, means, parts):
    count, first_height, depth = firsts.shape
    second_count, second_height, _ = seconds.shape
    scale = 1.0 / (rays * half)
    second_sum = jnp.concatenate(second_sums, axis=0)
    centers = []
    for n in range(count):
        center = jnp.sum(second_sum * first_sums[n], axis=1, keepdims=True) * scale
        means[:second_count, n * first_height : (n + 1) * first_height] = jnp.broadcast_to(
            center, (second_count, first_height)
        )
        centers.append(center)
    total = count * first_height
    for begin in range(0, total, CHUNK):
        end = min(begin + CHUNK, total)
        wanted = firsts[...].reshape(total, depth)[begin:end]
        for low in range(0, second_count, GROUP):
            size = min(GROUP, second_count - low)
            corr = lax.dot_general(
                seconds[low : low + size].reshape(size * second_height, depth),
                wanted,
                (((1,), (1,)), ((), ())),
                preferred_element_type=jnp.float32,
            )
            for m in range(low, low + size):
                values = corr[(m - low) * second_height : (m - low) * second_height + half]
                top = jnp.maximum(values, means[m : m + 1, begin:end])
                parts[m : m + 1, begin:end] = jnp.sum(top, axis=0, keepdims=True)
    spreads = []
    for n in range(count):
        part = parts[:second_count, n * first_height : n * first_height + rays] - half * centers[n]
        spreads.append(jnp.sum(part, axis=1, keepdims=True) * (2.0 * scale))
    return centers, spreads


def place(plan, ns, ms, centers, spreads, first_rows, second_rows, index, picked_first, picked_second):
    z, x, core, c = position()
    slot = (((x * plan.cols + c) * plan.depth) + z) * PAIR + core
    wide = (len(ms), plan.width)
    row = lax.broadcasted_iota(jnp.int32, wide, 0)
    second = jnp.zeros(wide, jnp.int32)
    for m, name in enumerate(ms):
        second = jnp.where(row == m, name, second)
    lane = lax.broadcasted_iota(jnp.int32, wide, 1)
    placed = jnp.zeros(wide, jnp.float32)
    for n, name in enumerate(ns):
        for m in range(len(ms)):
            which = name * plan.seconds + ms[m]
            picked_first[m : m + 1, :] = first_rows[n, pl.ds(index[0, which], 1), :]
            picked_second[m : m + 1, :] = second_rows[m, pl.ds(index[1, which], 1), :]
        picked = jnp.sum(picked_first[: len(ms)] * picked_second[: len(ms)], axis=1, keepdims=True)
        score = (picked - centers[n]) / (spreads[n] + 1e-05)
        placed = placed + jnp.where(lane == slot ^ (name * plan.seconds + second), score, 0.0)
    return jnp.sum(placed, axis=0, keepdims=True)


def early_kernel(rays, half, ns, ms, *refs):
    firsts, refs = refs[: len(ns)], refs[len(ns) :]
    seconds, refs = refs[: len(ms)], refs[len(ms) :]
    first_stack, first_rows, first_sum, second_stack, second_rows, second_sum, stats, means, parts = refs
    first_sums = load_firsts(firsts, first_stack, first_rows)
    second_sums = load_seconds(seconds, half, second_stack, second_rows)
    first_sum[...] = jnp.concatenate(first_sums, axis=0)
    second_sum[...] = jnp.concatenate(second_sums, axis=0)
    centers, spreads = cross(rays, half, first_stack, second_stack, first_sums, second_sums, means, parts)
    for n in range(len(ns)):
        stats[0, n] = jnp.broadcast_to(centers[n], (len(ms), LANES))
        stats[1, n] = jnp.broadcast_to(spreads[n], (len(ms), LANES))


def last_kernel(plan, rays, half, early, late, *refs):
    ns, ms = late
    firsts, refs = refs[: len(ns)], refs[len(ns) :]
    seconds, refs = refs[: len(ms)], refs[len(ms) :]
    early_firsts, early_rows, early_sum, early_seconds, early_second_rows, early_second_sum = refs[:6]
    early_stats, own_ref, start_ref, message_ref, index_row, index, sem = refs[6:13]
    first_stack, first_rows, second_stack, second_rows, means, parts, picked_first, picked_second = refs[13:]
    own_table = own_ref[0, rays : rays + TABLE]
    next_table = firsts[ns.index(plan.cols)][0, rays : rays + TABLE]
    paired, sent = lines(plan, own_table, next_table)
    index_row[0:1, : plan.pairs] = paired[0].astype(jnp.int32)
    index_row[1:2, : plan.pairs] = paired[1].astype(jnp.int32)
    copy = pltpu.make_async_copy(index_row, index, sem)
    copy.start()
    first_sums = load_firsts(firsts, first_stack, first_rows)
    second_sums = load_seconds(seconds, half, second_stack, second_rows)
    old_first_sums = [early_sum[n : n + 1] for n in range(len(early[0]))]
    old_second_sums = [early_second_sum[m : m + 1] for m in range(len(early[1]))]
    blocks = (
        (ns, early[1], first_rows, early_second_rows),
        (early[0], ms, early_rows, second_rows),
        (ns, ms, first_rows, second_rows),
        (early[0], early[1], early_rows, early_second_rows),
    )
    arrays = (
        (first_stack, early_seconds, first_sums, old_second_sums),
        (early_firsts, second_stack, old_first_sums, second_sums),
        (first_stack, second_stack, first_sums, second_sums),
    )
    stats = [cross(rays, half, *arrays[k], means.at[k], parts.at[k]) for k in range(3)]
    stats.append([[early_stats[kind, n][:, 0:1] for n in range(len(early[0]))] for kind in range(2)])
    copy.wait()
    spare = plan.width - 3 * plan.pairs - 9
    message = jnp.concatenate(
        [jnp.zeros((1, plan.pairs), jnp.float32), *sent, *(start_ref[k] for k in range(3))]
        + [jnp.zeros((1, spare), jnp.float32)] * (spare > 0),
        axis=1,
    )
    for k, (one, two, one_rows, two_rows) in enumerate(blocks):
        message = message + place(
            plan, one, two, *stats[k], one_rows, two_rows, index, picked_first.at[k], picked_second.at[k]
        )
    message_ref[...] = jnp.broadcast_to(message[None], message_ref.shape)


def power_kernel(plan, rays, gathered_ref, scores_ref, frames_ref, rows_ref, sorted_ref, matrix_ref):
    z, x, core, c = position()
    count, seconds = plan.count, plan.seconds
    for device in range(count):
        dz, rest = divmod(device, PAIR * PAIR * plan.cols)
        dx, rest = divmod(rest, PAIR * plan.cols)
        dk, dc = divmod(rest, plan.cols)
        rows_ref[pl.ds((dx * plan.cols + dc) * seconds + dz * PAIR + dk, 1), :] = gathered_ref[device]

    lane = lax.broadcasted_iota(jnp.int32, (seconds, plan.width), 1)
    block = (lane // seconds) % plan.firsts
    for to in range(plan.firsts):
        mixed = jnp.zeros((seconds, plan.width), jnp.float32)
        for b in range(plan.firsts):
            moved = rows_ref[b * seconds : (b + 1) * seconds, :]
            if b != to:
                moved = jnp.roll(moved, (b - to) * seconds, axis=1)
            mixed = jnp.where(block == b, moved, mixed)
        sorted_ref[to * seconds : (to + 1) * seconds, :] = mixed

    score = sorted_ref[:, :count]
    turn = 2.0 * math.pi / rays
    first = sorted_ref[:, count : 2 * count] * turn
    second = sorted_ref[:, 2 * count : 3 * count] * turn
    weighted = jnp.concatenate([score * jnp.cos(second), score * jnp.sin(second), score], axis=1)
    for p, unit in enumerate((jnp.cos(first), jnp.sin(first))):
        matrix_ref[p * count : (p + 1) * count, :] = weighted * jnp.concatenate([unit] * 3, axis=1)
    matrix_ref[2 * count :, :] = weighted

    begin = 3 * plan.pairs
    tile = begin // LANES * LANES
    turned = jnp.transpose(rows_ref[:, tile : tile + LANES])
    at = begin - tile
    frames = [
        jnp.concatenate([turned[at + 3 * k + q : at + 3 * k + q + 1] for q in range(3)], axis=1) for k in range(3)
    ]
    pad = jnp.zeros((5, 3 * count), jnp.float32)
    for _ in range(ITERS):
        stacked = jnp.concatenate(frames + [pad], axis=0)
        mixed = lax.dot_general(
            stacked,
            matrix_ref[...],
            (((1,), (1,)), ((), ())),
            precision=lax.Precision.HIGHEST,
            preferred_element_type=jnp.float32,
        )
        y = [mixed[k : k + 1] for k in range(3)]

        def gram(k, l):
            return jnp.sum(y[k] * y[l], axis=1, keepdims=True)

        f00 = jnp.sqrt(gram(0, 0))
        f10 = gram(1, 0) / f00
        f20 = gram(2, 0) / f00
        f11 = jnp.sqrt(gram(1, 1) - f10 * f10)
        f21 = (gram(2, 1) - f20 * f10) / f11
        f22 = jnp.sqrt(gram(2, 2) - f20 * f20 - f21 * f21)
        v0 = y[0] / f00
        v1 = (y[1] - f10 * v0) / f11
        v2 = (y[2] - f20 * v0 - f21 * v1) / f22
        frames = [v0, v1, v2]

    own = (x * plan.cols + c) * seconds + z * PAIR + core
    wide = lax.broadcasted_iota(jnp.int32, (1, 3 * count), 1)
    three = lax.broadcasted_iota(jnp.int32, (1, 3), 1)
    for k in range(3):
        out = jnp.zeros((1, 3), jnp.float32)
        for q in range(3):
            value = jnp.sum(jnp.where(wide == q * count + own, frames[k], 0.0), axis=1, keepdims=True)
            out = jnp.where(three == q, value, out)
        frames_ref[k] = math.sqrt(count) * out

    source = lax.broadcasted_iota(jnp.int32, (seconds, plan.rows), 0)
    target = lax.broadcasted_iota(jnp.int32, (seconds, plan.rows), 1)
    lines = [jnp.zeros((1, plan.rows), jnp.float32) for _ in range(plan.cols)]
    for dx in range(PAIR):
        row = rows_ref[pl.ds((dx * plan.cols + c) * seconds + z * PAIR + core, 1), :]
        spread = (target == (source // PAIR) * (PAIR * PAIR) + dx * PAIR + source % PAIR).astype(jnp.float32)
        for dc in range(plan.cols):
            low = row[:, dc * seconds : (dc + 1) * seconds]
            high = row[:, (plan.cols + dc) * seconds : (plan.cols + dc + 1) * seconds]
            part = jnp.broadcast_to(jnp.where(x == 1, high, low), (8, seconds))
            moved = lax.dot_general(
                part,
                spread,
                (((1,), (0,)), ((), ())),
                precision=lax.Precision.HIGHEST,
                preferred_element_type=jnp.float32,
            )
            lines[dc] = lines[dc] + moved[0:1]
    for dc in range(plan.cols):
        scores_ref[dc] = lines[dc]


def scored(plan, polar_rays, first_line, second_line, start_frame):
    _, rays, depth = polar_rays.shape
    half = rays // 2
    half_tiled = -(-half // 8) * 8
    axes = ("row", "col")
    vmem = pl.BlockSpec(memory_space=pltpu.VMEM)

    def swap(value, distance):
        return lax.ppermute(value, axes, [(n, n ^ distance) for n in range(plan.count)])

    first = jnp.transpose(first_line, (0, 2, 1))
    second = jnp.transpose(second_line, (0, 2, 1))
    start = jnp.transpose(start_frame, (0, 2, 1))
    inputs = [pltpu.with_memory_space_constraint(one, pltpu.HBM) for one in (polar_rays, first, second, start)]
    own_rays, half_rays, own_frame = pl.pallas_call(
        functools.partial(prepare_kernel, plan),
        out_shape=(
            jax.ShapeDtypeStruct((1, rays + TABLE, depth), polar_rays.dtype),
            jax.ShapeDtypeStruct((1, half_tiled, depth), polar_rays.dtype),
            jax.ShapeDtypeStruct(start.shape, start.dtype),
        ),
        in_specs=[pl.BlockSpec(memory_space=pltpu.HBM)] * 4,
        out_specs=(vmem, vmem, vmem),
        scratch_shapes=[
            pltpu.VMEM(first.shape, first.dtype),
            pltpu.VMEM(second.shape, second.dtype),
            pltpu.SemaphoreType.DMA((6,)),
        ],
        compiler_params=pltpu.CompilerParams(vmem_limit_bytes=1 << 20),
        name="prepare",
    )(*inputs)
    fulls = [own_rays] + [swap(own_rays, plan.flat(0, n // plan.cols, 0, n % plan.cols)) for n in range(1, plan.firsts)]
    deep = [half_rays] + [swap(half_rays, plan.flat(dz, 0, 0, 0)) for dz in range(1, plan.depth)]
    halves = []
    for piece in deep:
        halves += [piece, swap(piece, plan.flat(0, 0, 1, 0))]

    first_height, second_height = -(-rays // 16) * 16, -(-half // 16) * 16
    params = pltpu.CompilerParams(vmem_limit_bytes=SCORE_VMEM)
    (early_ns, early_ms), (late_ns, late_ms) = early_part(plan), late_part(plan)

    def stacks(ns, ms):
        return [
            ((len(ns), first_height, depth), polar_rays.dtype),
            ((len(ns), rays, depth), jnp.float32),
            ((len(ns), depth), jnp.float32),
            ((len(ms), second_height, depth), polar_rays.dtype),
            ((len(ms), half, depth), jnp.float32),
            ((len(ms), depth), jnp.float32),
        ]

    most = max(len(early_ms), len(late_ms))
    span = max(len(early_ns), len(late_ns)) * first_height
    before = pl.pallas_call(
        functools.partial(early_kernel, rays, half, early_ns, early_ms),
        out_shape=[jax.ShapeDtypeStruct(*one) for one in stacks(early_ns, early_ms)]
        + [jax.ShapeDtypeStruct((2, len(early_ns), len(early_ms), LANES), jnp.float32)],
        in_specs=[vmem] * (len(early_ns) + len(early_ms)),
        out_specs=[vmem] * 7,
        compiler_params=params,
        scratch_shapes=[pltpu.VMEM((most, span), jnp.float32)] * 2,
        name="early",
    )(*(fulls[n] for n in early_ns), *(halves[m] for m in early_ms))
    new = stacks(late_ns, late_ms)
    message = pl.pallas_call(
        functools.partial(last_kernel, plan, rays, half, (early_ns, early_ms), (late_ns, late_ms)),
        out_shape=jax.ShapeDtypeStruct((plan.count, 1, plan.width), jnp.float32),
        in_specs=[vmem] * (len(late_ns) + len(late_ms) + 9),
        out_specs=vmem,
        compiler_params=params,
        scratch_shapes=[
            pltpu.VMEM((2, plan.index), jnp.int32),
            pltpu.SMEM((2, plan.index), jnp.int32),
            pltpu.SemaphoreType.DMA,
        ]
        + [pltpu.VMEM(*one) for one in (new[0], new[1], new[3], new[4])]
        + [pltpu.VMEM((3, most, span), jnp.float32)] * 2
        + [pltpu.VMEM((4, most, depth), jnp.float32)] * 2,
        name="last",
    )(*(fulls[n] for n in late_ns), *(halves[m] for m in late_ms), *before, own_rays, own_frame)

    gathered = lax.all_to_all(message, axes, 0, 0, tiled=True)

    scores, frames = pl.pallas_call(
        functools.partial(power_kernel, plan, rays),
        out_shape=(
            jax.ShapeDtypeStruct((plan.cols, 1, plan.rows), jnp.float32),
            jax.ShapeDtypeStruct((3, 1, 3), jnp.float32),
        ),
        in_specs=[vmem],
        out_specs=(vmem, vmem),
        compiler_params=pltpu.CompilerParams(vmem_limit_bytes=POWER_VMEM),
        scratch_shapes=[
            pltpu.VMEM((plan.count, plan.width), jnp.float32),
            pltpu.VMEM((plan.count, plan.width), jnp.float32),
            pltpu.VMEM((3 * plan.count, 3 * plan.count), jnp.float32),
        ],
        name="power",
    )(gathered)
    return jnp.transpose(scores, (0, 2, 1)), jnp.transpose(frames, (0, 2, 1))


def per_device(plan, *arrays):
    return scored(plan, *arrays)


def early_part(plan):
    deep = [0] + list(range(plan.depth - 1, plan.depth // 2, -1))
    return (0, plan.firsts - 1), tuple(PAIR * dz + dk for dz in deep for dk in range(PAIR))


def late_part(plan):
    ns, ms = early_part(plan)
    return (
        tuple(n for n in range(plan.firsts) if n not in ns),
        tuple(m for m in range(plan.seconds) if m not in ms),
    )


def solution(mesh):
    plan = Plan(mesh.shape["row"], mesh.shape["col"])
    placed = (
        P(("row", "col"), None, None),
        P("row", None, "col"),
        P("row", None, "col"),
        P(None, None, ("row", "col")),
    )
    return jax.shard_map(
        functools.partial(per_device, plan),
        mesh=mesh,
        in_specs=placed,
        out_specs=(P("row", None, "col"), P(None, None, ("row", "col"))),
        check_vma=False,
    )
```

```python
import functools
import math

import jax
import jax.numpy as jnp
from jax import lax
from jax.experimental import pallas as pl
from jax.experimental.pallas import tpu as pltpu
from jax.sharding import PartitionSpec as P

ITERS = 3
LANES = 128
TABLE = 8
CHUNK = 256
GROUP = 8
SCORE_VMEM = 24 << 20
POWER_VMEM = 16 << 20
PAIR = 2


class Plan:
    def __init__(self, rows, cols):
        self.rows, self.cols = rows, cols
        self.depth = rows // (PAIR * PAIR)
        self.count = rows * cols
        self.firsts = PAIR * cols
        self.seconds = PAIR * self.depth
        self.pairs = self.firsts * self.seconds
        self.width = -(-(3 * self.pairs + 9) // LANES) * LANES
        self.index = -(-self.pairs // LANES) * LANES

    def flat(self, z, x, core, c):
        return ((z * PAIR + x) * PAIR + core) * self.cols + c


def position():
    row, c = lax.axis_index("row"), lax.axis_index("col")
    return row // (PAIR * PAIR), (row // PAIR) % PAIR, row % PAIR, c


def prepare_kernel(
    plan, rays_ref, first_ref, second_ref, start_ref, full_ref, half_ref, frame_ref, first_row, second_row, sems
):
    rays, depth = rays_ref.shape[1:]
    half = half_ref.shape[1]
    moves = (
        (rays_ref.at[:, pl.ds(0, half)], half_ref),
        (rays_ref.at[:, pl.ds(0, half)], full_ref.at[:, pl.ds(0, half)]),
        (rays_ref.at[:, pl.ds(half, rays - half)], full_ref.at[:, pl.ds(half, rays - half)]),
        (first_ref, first_row),
        (second_ref, second_row),
        (start_ref, frame_ref),
    )
    copies = [pltpu.make_async_copy(*move, sems.at[k]) for k, move in enumerate(moves)]
    for copy in copies:
        copy.start()
    for copy in copies:
        copy.wait()

    def row(table_ref):
        parts = [table_ref[c] for c in range(plan.cols)]
        spare = depth - plan.rows * plan.cols
        return jnp.concatenate(parts + [jnp.zeros((1, spare), jnp.int32)] * (spare > 0), axis=1)

    first, second = row(first_row), row(second_row)
    rows = jnp.concatenate([first >> 1, first & 1, second, jnp.zeros((TABLE - 3, depth), jnp.int32)], axis=0)
    full_ref[0, rays : rays + TABLE] = rows.astype(jnp.float32).astype(full_ref.dtype)


def pick_lines(own_table, next_table, own_at, next_at):
    chosen = 0.0
    for table, at in ((own_table, own_at), (next_table, next_at)):
        column = lax.broadcasted_iota(jnp.int32, (table.shape[1], at.shape[1]), 0)
        here = jnp.where(column == at, 1.0, 0.0).astype(table.dtype)
        chosen = chosen + jnp.dot(table, here, preferred_element_type=jnp.float32)
    return 2.0 * chosen[0:1] + chosen[1:2], chosen[2:3]


def lines(plan, own_table, next_table):
    z, x, core, c = position()
    number = lax.broadcasted_iota(jnp.int32, (1, plan.pairs), 1)
    dk, rest = number % PAIR, number // PAIR
    dz, rest = rest % plan.depth, rest // plan.depth
    dc, dx = rest % plan.cols, rest // plan.cols
    at = (c ^ dc) * plan.rows + ((z ^ dz) * PAIR + x) * PAIR + (core ^ dk)
    paired = pick_lines(own_table, next_table, jnp.where(dx == 0, at, -1), jnp.where(dx == 0, -1, at))
    at = dc * plan.rows + (dz * PAIR + x) * PAIR + dk
    sent = pick_lines(own_table, next_table, jnp.where(dx == x, at, -1), jnp.where(dx == x, -1, at))
    return paired, sent


def load_firsts(refs, stack, rows):
    sums = []
    for n, ref in enumerate(refs):
        stack[n, : ref.shape[1]] = ref[0]
        values = ref[0, : rows.shape[1]].astype(jnp.float32)
        rows[n] = values
        sums.append(jnp.sum(values, axis=0, keepdims=True))
    return sums


def load_seconds(refs, half, stack, rows):
    sums = []
    for m, ref in enumerate(refs):
        stack[m, : ref.shape[1]] = ref[0]
        values = ref[0, :half].astype(jnp.float32)
        rows[m] = values
        sums.append(jnp.sum(values, axis=0, keepdims=True))
    return sums


def cross(rays, half, firsts, seconds, first_sums, second_sums, means, parts):
    count, first_height, depth = firsts.shape
    second_count, second_height, _ = seconds.shape
    scale = 1.0 / (rays * half)
    second_sum = jnp.concatenate(second_sums, axis=0)
    centers = []
    for n in range(count):
        center = jnp.sum(second_sum * first_sums[n], axis=1, keepdims=True) * scale
        means[:second_count, n * first_height : (n + 1) * first_height] = jnp.broadcast_to(
            center, (second_count, first_height)
        )
        centers.append(center)
    total = count * first_height
    for begin in range(0, total, CHUNK):
        end = min(begin + CHUNK, total)
        wanted = firsts[...].reshape(total, depth)[begin:end]
        for low in range(0, second_count, GROUP):
            size = min(GROUP, second_count - low)
            corr = lax.dot_general(
                seconds[low : low + size].reshape(size * second_height, depth),
                wanted,
                (((1,), (1,)), ((), ())),
                preferred_element_type=jnp.float32,
            )
            for m in range(low, low + size):
                values = corr[(m - low) * second_height : (m - low) * second_height + half]
                top = jnp.maximum(values, means[m : m + 1, begin:end])
                parts[m : m + 1, begin:end] = jnp.sum(top, axis=0, keepdims=True)
    spreads = []
    for n in range(count):
        part = parts[:second_count, n * first_height : n * first_height + rays] - half * centers[n]
        spreads.append(jnp.sum(part, axis=1, keepdims=True) * (2.0 * scale))
    return centers, spreads


def place(plan, ns, ms, centers, spreads, first_rows, second_rows, index, picked_first, picked_second):
    z, x, core, c = position()
    slot = (((x * plan.cols + c) * plan.depth) + z) * PAIR + core
    wide = (len(ms), plan.width)
    row = lax.broadcasted_iota(jnp.int32, wide, 0)
    second = jnp.zeros(wide, jnp.int32)
    for m, name in enumerate(ms):
        second = jnp.where(row == m, name, second)
    lane = lax.broadcasted_iota(jnp.int32, wide, 1)
    placed = jnp.zeros(wide, jnp.float32)
    for n, name in enumerate(ns):
        for m in range(len(ms)):
            which = name * plan.seconds + ms[m]
            picked_first[m : m + 1, :] = first_rows[n, pl.ds(index[0, which], 1), :]
            picked_second[m : m + 1, :] = second_rows[m, pl.ds(index[1, which], 1), :]
        picked = jnp.sum(picked_first[: len(ms)] * picked_second[: len(ms)], axis=1, keepdims=True)
        score = (picked - centers[n]) / (spreads[n] + 1e-05)
        placed = placed + jnp.where(lane == slot ^ (name * plan.seconds + second), score, 0.0)
    return jnp.sum(placed, axis=0, keepdims=True)


def early_kernel(rays, half, ns, ms, *refs):
    firsts, refs = refs[: len(ns)], refs[len(ns) :]
    seconds, refs = refs[: len(ms)], refs[len(ms) :]
    first_stack, first_rows, first_sum, second_stack, second_rows, second_sum, stats, means, parts = refs
    first_sums = load_firsts(firsts, first_stack, first_rows)
    second_sums = load_seconds(seconds, half, second_stack, second_rows)
    first_sum[...] = jnp.concatenate(first_sums, axis=0)
    second_sum[...] = jnp.concatenate(second_sums, axis=0)
    centers, spreads = cross(rays, half, first_stack, second_stack, first_sums, second_sums, means, parts)
    for n in range(len(ns)):
        stats[0, n] = jnp.broadcast_to(centers[n], (len(ms), LANES))
        stats[1, n] = jnp.broadcast_to(spreads[n], (len(ms), LANES))


def last_kernel(plan, rays, half, early, late, *refs):
    ns, ms = late
    firsts, refs = refs[: len(ns)], refs[len(ns) :]
    seconds, refs = refs[: len(ms)], refs[len(ms) :]
    early_firsts, early_rows, early_sum, early_seconds, early_second_rows, early_second_sum = refs[:6]
    early_stats, own_ref, start_ref, message_ref, index_row, index, sem = refs[6:13]
    first_stack, first_rows, second_stack, second_rows, means, parts, picked_first, picked_second = refs[13:]
    own_table = own_ref[0, rays : rays + TABLE]
    next_table = firsts[ns.index(plan.cols)][0, rays : rays + TABLE]
    paired, sent = lines(plan, own_table, next_table)
    index_row[0:1, : plan.pairs] = paired[0].astype(jnp.int32)
    index_row[1:2, : plan.pairs] = paired[1].astype(jnp.int32)
    copy = pltpu.make_async_copy(index_row, index, sem)
    copy.start()
    first_sums = load_firsts(firsts, first_stack, first_rows)
    second_sums = load_seconds(seconds, half, second_stack, second_rows)
    old_first_sums = [early_sum[n : n + 1] for n in range(len(early[0]))]
    old_second_sums = [early_second_sum[m : m + 1] for m in range(len(early[1]))]
    blocks = (
        (ns, early[1], first_rows, early_second_rows),
        (early[0], ms, early_rows, second_rows),
        (ns, ms, first_rows, second_rows),
        (early[0], early[1], early_rows, early_second_rows),
    )
    arrays = (
        (first_stack, early_seconds, first_sums, old_second_sums),
        (early_firsts, second_stack, old_first_sums, second_sums),
        (first_stack, second_stack, first_sums, second_sums),
    )
    stats = [cross(rays, half, *arrays[k], means.at[k], parts.at[k]) for k in range(3)]
    stats.append([[early_stats[kind, n][:, 0:1] for n in range(len(early[0]))] for kind in range(2)])
    copy.wait()
    spare = plan.width - 3 * plan.pairs - 9
    message = jnp.concatenate(
        [jnp.zeros((1, plan.pairs), jnp.float32), *sent, *(start_ref[k] for k in range(3))]
        + [jnp.zeros((1, spare), jnp.float32)] * (spare > 0),
        axis=1,
    )
    for k, (one, two, one_rows, two_rows) in enumerate(blocks):
        message = message + place(
            plan, one, two, *stats[k], one_rows, two_rows, index, picked_first.at[k], picked_second.at[k]
        )
    message_ref[...] = jnp.broadcast_to(message[None], message_ref.shape)


def power_kernel(plan, rays, gathered_ref, scores_ref, frames_ref, rows_ref, sorted_ref, matrix_ref):
    z, x, core, c = position()
    count, seconds = plan.count, plan.seconds
    for device in range(count):
        dz, rest = divmod(device, PAIR * PAIR * plan.cols)
        dx, rest = divmod(rest, PAIR * plan.cols)
        dk, dc = divmod(rest, plan.cols)
        rows_ref[pl.ds((dx * plan.cols + dc) * seconds + dz * PAIR + dk, 1), :] = gathered_ref[device]

    lane = lax.broadcasted_iota(jnp.int32, (seconds, plan.width), 1)
    block = (lane // seconds) % plan.firsts
    for to in range(plan.firsts):
        mixed = jnp.zeros((seconds, plan.width), jnp.float32)
        for b in range(plan.firsts):
            moved = rows_ref[b * seconds : (b + 1) * seconds, :]
            if b != to:
                moved = jnp.roll(moved, (b - to) * seconds, axis=1)
            mixed = jnp.where(block == b, moved, mixed)
        sorted_ref[to * seconds : (to + 1) * seconds, :] = mixed

    score = sorted_ref[:, :count]
    turn = 2.0 * math.pi / rays
    first = sorted_ref[:, count : 2 * count] * turn
    second = sorted_ref[:, 2 * count : 3 * count] * turn
    weighted = jnp.concatenate([score * jnp.cos(second), score * jnp.sin(second), score], axis=1)
    for p, unit in enumerate((jnp.cos(first), jnp.sin(first))):
        matrix_ref[p * count : (p + 1) * count, :] = weighted * jnp.concatenate([unit] * 3, axis=1)
    matrix_ref[2 * count :, :] = weighted

    begin = 3 * plan.pairs
    tile = begin // LANES * LANES
    turned = jnp.transpose(rows_ref[:, tile : tile + LANES])
    at = begin - tile
    frames = [
        jnp.concatenate([turned[at + 3 * k + q : at + 3 * k + q + 1] for q in range(3)], axis=1) for k in range(3)
    ]
    pad = jnp.zeros((5, 3 * count), jnp.float32)

    def applied(values):
        mixed = lax.dot_general(
            jnp.concatenate(values + [pad], axis=0),
            matrix_ref[...],
            (((1,), (1,)), ((), ())),
            precision=lax.Precision.HIGHEST,
            preferred_element_type=jnp.float32,
        )
        return [mixed[k : k + 1] for k in range(3)]

    def factor(y):
        g00, g10, g20, g11, g21, g22 = (
            jnp.sum(y[k] * y[l], axis=1, keepdims=True) for k, l in ((0, 0), (1, 0), (2, 0), (1, 1), (2, 1), (2, 2))
        )
        r0 = lax.rsqrt(g00)
        f10, f20 = g10 * r0, g20 * r0
        r1 = lax.rsqrt(g11 - f10 * f10)
        f21 = (g21 - f20 * f10) * r1
        r2 = lax.rsqrt(g22 - f20 * f20 - f21 * f21)
        return f10, f20, f21, r0, r1, r2

    def solved(parts, y):
        f10, f20, f21, r0, r1, r2 = parts
        v0 = y[0] * r0
        v1 = (y[1] - f10 * v0) * r1
        return [v0, v1, (y[2] - f20 * v0 - f21 * v1) * r2]

    y = applied(frames)
    for _ in range(ITERS - 1):
        y = solved(factor(y), applied(y))
    frames = solved(factor(y), y)

    own = (x * plan.cols + c) * seconds + z * PAIR + core
    wide = lax.broadcasted_iota(jnp.int32, (1, 3 * count), 1)
    three = lax.broadcasted_iota(jnp.int32, (1, 3), 1)
    for k in range(3):
        out = jnp.zeros((1, 3), jnp.float32)
        for q in range(3):
            value = jnp.sum(jnp.where(wide == q * count + own, frames[k], 0.0), axis=1, keepdims=True)
            out = jnp.where(three == q, value, out)
        frames_ref[k] = math.sqrt(count) * out

    source = lax.broadcasted_iota(jnp.int32, (seconds, plan.rows), 0)
    target = lax.broadcasted_iota(jnp.int32, (seconds, plan.rows), 1)
    lines = [jnp.zeros((1, plan.rows), jnp.float32) for _ in range(plan.cols)]
    for dx in range(PAIR):
        row = rows_ref[pl.ds((dx * plan.cols + c) * seconds + z * PAIR + core, 1), :]
        spread = (target == (source // PAIR) * (PAIR * PAIR) + dx * PAIR + source % PAIR).astype(jnp.float32)
        for dc in range(plan.cols):
            low = row[:, dc * seconds : (dc + 1) * seconds]
            high = row[:, (plan.cols + dc) * seconds : (plan.cols + dc + 1) * seconds]
            part = jnp.broadcast_to(jnp.where(x == 1, high, low), (8, seconds))
            moved = lax.dot_general(
                part,
                spread,
                (((1,), (0,)), ((), ())),
                precision=lax.Precision.HIGHEST,
                preferred_element_type=jnp.float32,
            )
            lines[dc] = lines[dc] + moved[0:1]
    for dc in range(plan.cols):
        scores_ref[dc] = lines[dc]


def scored(plan, polar_rays, first_line, second_line, start_frame):
    _, rays, depth = polar_rays.shape
    half = rays // 2
    half_tiled = -(-half // 8) * 8
    axes = ("row", "col")
    vmem = pl.BlockSpec(memory_space=pltpu.VMEM)

    def swap(value, distance):
        return lax.ppermute(value, axes, [(n, n ^ distance) for n in range(plan.count)])

    first = jnp.transpose(first_line, (0, 2, 1))
    second = jnp.transpose(second_line, (0, 2, 1))
    start = jnp.transpose(start_frame, (0, 2, 1))
    inputs = [pltpu.with_memory_space_constraint(one, pltpu.HBM) for one in (polar_rays, first, second, start)]
    own_rays, half_rays, own_frame = pl.pallas_call(
        functools.partial(prepare_kernel, plan),
        out_shape=(
            jax.ShapeDtypeStruct((1, rays + TABLE, depth), polar_rays.dtype),
            jax.ShapeDtypeStruct((1, half_tiled, depth), polar_rays.dtype),
            jax.ShapeDtypeStruct(start.shape, start.dtype),
        ),
        in_specs=[pl.BlockSpec(memory_space=pltpu.HBM)] * 4,
        out_specs=(vmem, vmem, vmem),
        scratch_shapes=[
            pltpu.VMEM(first.shape, first.dtype),
            pltpu.VMEM(second.shape, second.dtype),
            pltpu.SemaphoreType.DMA((6,)),
        ],
        compiler_params=pltpu.CompilerParams(vmem_limit_bytes=1 << 20),
        name="prepare",
    )(*inputs)
    fulls = [own_rays] + [swap(own_rays, plan.flat(0, n // plan.cols, 0, n % plan.cols)) for n in range(1, plan.firsts)]
    deep = [half_rays] + [swap(half_rays, plan.flat(dz, 0, 0, 0)) for dz in range(1, plan.depth)]
    halves = []
    for piece in deep:
        halves += [piece, swap(piece, plan.flat(0, 0, 1, 0))]

    first_height, second_height = -(-rays // 16) * 16, -(-half // 16) * 16
    params = pltpu.CompilerParams(vmem_limit_bytes=SCORE_VMEM)
    (early_ns, early_ms), (late_ns, late_ms) = early_part(plan), late_part(plan)

    def stacks(ns, ms):
        return [
            ((len(ns), first_height, depth), polar_rays.dtype),
            ((len(ns), rays, depth), jnp.float32),
            ((len(ns), depth), jnp.float32),
            ((len(ms), second_height, depth), polar_rays.dtype),
            ((len(ms), half, depth), jnp.float32),
            ((len(ms), depth), jnp.float32),
        ]

    most = max(len(early_ms), len(late_ms))
    span = max(len(early_ns), len(late_ns)) * first_height
    before = pl.pallas_call(
        functools.partial(early_kernel, rays, half, early_ns, early_ms),
        out_shape=[jax.ShapeDtypeStruct(*one) for one in stacks(early_ns, early_ms)]
        + [jax.ShapeDtypeStruct((2, len(early_ns), len(early_ms), LANES), jnp.float32)],
        in_specs=[vmem] * (len(early_ns) + len(early_ms)),
        out_specs=[vmem] * 7,
        compiler_params=params,
        scratch_shapes=[pltpu.VMEM((most, span), jnp.float32)] * 2,
        name="early",
    )(*(fulls[n] for n in early_ns), *(halves[m] for m in early_ms))
    new = stacks(late_ns, late_ms)
    message = pl.pallas_call(
        functools.partial(last_kernel, plan, rays, half, (early_ns, early_ms), (late_ns, late_ms)),
        out_shape=jax.ShapeDtypeStruct((plan.count, 1, plan.width), jnp.float32),
        in_specs=[vmem] * (len(late_ns) + len(late_ms) + 9),
        out_specs=vmem,
        compiler_params=params,
        scratch_shapes=[
            pltpu.VMEM((2, plan.index), jnp.int32),
            pltpu.SMEM((2, plan.index), jnp.int32),
            pltpu.SemaphoreType.DMA,
        ]
        + [pltpu.VMEM(*one) for one in (new[0], new[1], new[3], new[4])]
        + [pltpu.VMEM((3, most, span), jnp.float32)] * 2
        + [pltpu.VMEM((4, most, depth), jnp.float32)] * 2,
        name="last",
    )(*(fulls[n] for n in late_ns), *(halves[m] for m in late_ms), *before, own_rays, own_frame)

    gathered = lax.all_to_all(message, axes, 0, 0, tiled=True)

    scores, frames = pl.pallas_call(
        functools.partial(power_kernel, plan, rays),
        out_shape=(
            jax.ShapeDtypeStruct((plan.cols, 1, plan.rows), jnp.float32),
            jax.ShapeDtypeStruct((3, 1, 3), jnp.float32),
        ),
        in_specs=[vmem],
        out_specs=(vmem, vmem),
        compiler_params=pltpu.CompilerParams(vmem_limit_bytes=POWER_VMEM),
        scratch_shapes=[
            pltpu.VMEM((plan.count, plan.width), jnp.float32),
            pltpu.VMEM((plan.count, plan.width), jnp.float32),
            pltpu.VMEM((3 * plan.count, 3 * plan.count), jnp.float32),
        ],
        name="power",
    )(gathered)
    return jnp.transpose(scores, (0, 2, 1)), jnp.transpose(frames, (0, 2, 1))


def per_device(plan, *arrays):
    return scored(plan, *arrays)


def early_part(plan):
    deep = [0] + list(range(plan.depth - 1, plan.depth // 2, -1))
    return (0, plan.firsts - 1), tuple(PAIR * dz + dk for dz in deep for dk in range(PAIR))


def late_part(plan):
    ns, ms = early_part(plan)
    return (
        tuple(n for n in range(plan.firsts) if n not in ns),
        tuple(m for m in range(plan.seconds) if m not in ms),
    )


def solution(mesh):
    plan = Plan(mesh.shape["row"], mesh.shape["col"])
    placed = (
        P(("row", "col"), None, None),
        P("row", None, "col"),
        P("row", None, "col"),
        P(None, None, ("row", "col")),
    )
    return jax.shard_map(
        functools.partial(per_device, plan),
        mesh=mesh,
        in_specs=placed,
        out_specs=(P("row", None, "col"), P(None, None, ("row", "col"))),
        check_vma=False,
    )
```

```python
import functools
import math

import jax
import jax.numpy as jnp
from jax import lax
from jax.experimental import pallas as pl
from jax.experimental.pallas import tpu as pltpu
from jax.sharding import PartitionSpec as P

ITERS = 3
LANES = 128
TABLE = 8
CHUNK = 256
GROUP = 8
SCORE_VMEM = 24 << 20
POWER_VMEM = 16 << 20
PAIR = 2


class Plan:
    def __init__(self, rows, cols):
        self.rows, self.cols = rows, cols
        self.depth = rows // (PAIR * PAIR)
        self.count = rows * cols
        self.firsts = PAIR * cols
        self.seconds = PAIR * self.depth
        self.pairs = self.firsts * self.seconds
        self.width = -(-(3 * self.pairs + 9) // LANES) * LANES
        self.index = -(-self.pairs // LANES) * LANES

    def flat(self, z, x, core, c):
        return ((z * PAIR + x) * PAIR + core) * self.cols + c


def position():
    row, c = lax.axis_index("row"), lax.axis_index("col")
    return row // (PAIR * PAIR), (row // PAIR) % PAIR, row % PAIR, c


def prepare_kernel(
    plan, rays_ref, first_ref, second_ref, start_ref, full_ref, half_ref, frame_ref, first_row, second_row, sems
):
    rays, depth = rays_ref.shape[1:]
    half = half_ref.shape[1]
    cuts = [0, half // 16 * 8, half, half + (rays - half) // 16 * 8, rays]
    moves = [
        (rays_ref.at[:, pl.ds(low, high - low)], to.at[:, pl.ds(low, high - low)])
        for low, high, to in zip(cuts, cuts[1:], (half_ref, half_ref, full_ref, full_ref))
    ]
    moves += [(first_ref, first_row), (second_ref, second_row), (start_ref, frame_ref)]
    copies = [pltpu.make_async_copy(*move, sems.at[k]) for k, move in enumerate(moves)]
    for copy in copies:
        copy.start()
    for copy in copies:
        copy.wait()

    full_ref[0, :half] = half_ref[0]

    def row(table_ref):
        parts = [table_ref[c] for c in range(plan.cols)]
        spare = depth - plan.rows * plan.cols
        return jnp.concatenate(parts + [jnp.zeros((1, spare), jnp.int32)] * (spare > 0), axis=1)

    first, second = row(first_row), row(second_row)
    rows = jnp.concatenate([first >> 1, first & 1, second, jnp.zeros((TABLE - 3, depth), jnp.int32)], axis=0)
    full_ref[0, rays : rays + TABLE] = rows.astype(jnp.float32).astype(full_ref.dtype)


def pick_lines(own_table, next_table, own_at, next_at):
    chosen = 0.0
    for table, at in ((own_table, own_at), (next_table, next_at)):
        column = lax.broadcasted_iota(jnp.int32, (table.shape[1], at.shape[1]), 0)
        here = jnp.where(column == at, 1.0, 0.0).astype(table.dtype)
        chosen = chosen + jnp.dot(table, here, preferred_element_type=jnp.float32)
    return 2.0 * chosen[0:1] + chosen[1:2], chosen[2:3]


def lines(plan, own_table, next_table):
    z, x, core, c = position()
    number = lax.broadcasted_iota(jnp.int32, (1, plan.pairs), 1)
    dk, rest = number % PAIR, number // PAIR
    dz, rest = rest % plan.depth, rest // plan.depth
    dc, dx = rest % plan.cols, rest // plan.cols
    at = (c ^ dc) * plan.rows + ((z ^ dz) * PAIR + x) * PAIR + (core ^ dk)
    paired = pick_lines(own_table, next_table, jnp.where(dx == 0, at, -1), jnp.where(dx == 0, -1, at))
    at = dc * plan.rows + (dz * PAIR + x) * PAIR + dk
    sent = pick_lines(own_table, next_table, jnp.where(dx == x, at, -1), jnp.where(dx == x, -1, at))
    return paired, sent


def load_firsts(refs, stack, rows):
    sums = []
    for n, ref in enumerate(refs):
        stack[n, : ref.shape[1]] = ref[0]
        values = ref[0, : rows.shape[1]].astype(jnp.float32)
        rows[n] = values
        sums.append(jnp.sum(values, axis=0, keepdims=True))
    return sums


def load_seconds(refs, half, stack, rows):
    sums = []
    for m, ref in enumerate(refs):
        stack[m, : ref.shape[1]] = ref[0]
        values = ref[0, :half].astype(jnp.float32)
        rows[m] = values
        sums.append(jnp.sum(values, axis=0, keepdims=True))
    return sums


def cross(rays, half, firsts, seconds, first_sums, second_sums, means, parts):
    count, first_height, depth = firsts.shape
    second_count, second_height, _ = seconds.shape
    scale = 1.0 / (rays * half)
    second_sum = jnp.concatenate(second_sums, axis=0)
    centers = []
    for n in range(count):
        center = jnp.sum(second_sum * first_sums[n], axis=1, keepdims=True) * scale
        means[:second_count, n * first_height : (n + 1) * first_height] = jnp.broadcast_to(
            center, (second_count, first_height)
        )
        centers.append(center)
    total = count * first_height
    for begin in range(0, total, CHUNK):
        end = min(begin + CHUNK, total)
        wanted = firsts[...].reshape(total, depth)[begin:end]
        for low in range(0, second_count, GROUP):
            size = min(GROUP, second_count - low)
            corr = lax.dot_general(
                seconds[low : low + size].reshape(size * second_height, depth),
                wanted,
                (((1,), (1,)), ((), ())),
                preferred_element_type=jnp.float32,
            )
            for m in range(low, low + size):
                values = corr[(m - low) * second_height : (m - low) * second_height + half]
                top = jnp.maximum(values, means[m : m + 1, begin:end])
                parts[m : m + 1, begin:end] = jnp.sum(top, axis=0, keepdims=True)
    spreads = []
    for n in range(count):
        part = parts[:second_count, n * first_height : n * first_height + rays] - half * centers[n]
        spreads.append(jnp.sum(part, axis=1, keepdims=True) * (2.0 * scale))
    return centers, spreads


def place(plan, ns, ms, centers, spreads, first_rows, second_rows, index, picked_first, picked_second):
    z, x, core, c = position()
    slot = (((x * plan.cols + c) * plan.depth) + z) * PAIR + core
    wide = (len(ms), plan.width)
    row = lax.broadcasted_iota(jnp.int32, wide, 0)
    second = jnp.zeros(wide, jnp.int32)
    for m, name in enumerate(ms):
        second = jnp.where(row == m, name, second)
    lane = lax.broadcasted_iota(jnp.int32, wide, 1)
    placed = jnp.zeros(wide, jnp.float32)
    for n, name in enumerate(ns):
        for m in range(len(ms)):
            which = name * plan.seconds + ms[m]
            picked_first[m : m + 1, :] = first_rows[n, pl.ds(index[0, which], 1), :]
            picked_second[m : m + 1, :] = second_rows[m, pl.ds(index[1, which], 1), :]
        picked = jnp.sum(picked_first[: len(ms)] * picked_second[: len(ms)], axis=1, keepdims=True)
        score = (picked - centers[n]) / (spreads[n] + 1e-05)
        placed = placed + jnp.where(lane == slot ^ (name * plan.seconds + second), score, 0.0)
    return jnp.sum(placed, axis=0, keepdims=True)


def early_kernel(plan, rays, half, ns, ms, loaded, *refs):
    firsts, refs = refs[: len(ns)], refs[len(ns) :]
    if loaded:
        second_stack, second_sum, own_ref, start_ref = refs[:4]
        first_stack, first_rows, first_sum, stats, index_ref, base_ref, means, parts = refs[4:]
        tables = (ref[0, rays : rays + TABLE] for ref in (own_ref, firsts[ns.index(plan.cols)]))
        paired, sent = lines(plan, *tables)
        index_ref[0:1, : plan.pairs] = paired[0].astype(jnp.int32)
        index_ref[1:2, : plan.pairs] = paired[1].astype(jnp.int32)
        spare = plan.width - 3 * plan.pairs - 9
        base_ref[...] = jnp.concatenate(
            [jnp.zeros((1, plan.pairs), jnp.float32), *sent, *(start_ref[k] for k in range(3))]
            + [jnp.zeros((1, spare), jnp.float32)] * (spare > 0),
            axis=1,
        )
        second_sums = [second_sum[m : m + 1] for m in range(len(ms))]
    else:
        seconds, refs = refs[: len(ms)], refs[len(ms) :]
        first_stack, first_rows, first_sum, stats, second_stack, second_rows, second_sum, means, parts = refs
        second_sums = load_seconds(seconds, half, second_stack, second_rows)
        second_sum[...] = jnp.concatenate(second_sums, axis=0)
    first_sums = load_firsts(firsts, first_stack, first_rows)
    first_sum[...] = jnp.concatenate(first_sums, axis=0)
    centers, spreads = cross(rays, half, first_stack, second_stack, first_sums, second_sums, means, parts)
    for n in range(len(ns)):
        stats[0, n] = jnp.broadcast_to(centers[n], (len(ms), LANES))
        stats[1, n] = jnp.broadcast_to(spreads[n], (len(ms), LANES))


def last_kernel(plan, rays, half, groups, early, ns, ms, *refs):
    firsts, refs = refs[: len(ns)], refs[len(ns) :]
    seconds, refs = refs[: len(ms)], refs[len(ms) :]
    before, refs = [refs[4 * g : 4 * g + 4] for g in range(len(groups))], refs[4 * len(groups) :]
    early_seconds, early_second_rows, early_second_sum = refs[:3]
    index_ref, base_ref, message_ref, index, sem = refs[3:8]
    first_stack, first_rows, second_stack, second_rows, means, parts, picked_first, picked_second = refs[8:]
    copy = pltpu.make_async_copy(index_ref, index, sem)
    copy.start()
    second_sums = load_seconds(seconds, half, second_stack, second_rows)
    first_sums = load_firsts(firsts, first_stack, first_rows)
    old_second_sums = [early_second_sum[m : m + 1] for m in range(len(early))]

    blocks, stats = [], []

    def block(one, two, one_stack, two_stack, one_sums, two_sums, one_rows, two_rows):
        k = len(blocks)
        stats.append(cross(rays, half, one_stack, two_stack, one_sums, two_sums, means.at[k], parts.at[k]))
        blocks.append((one, two, one_rows, two_rows))

    for group, (stack, rows, sums, _) in zip(groups, before):
        old_sums = [sums[n : n + 1] for n in range(len(group))]
        block(group, ms, stack, second_stack, old_sums, second_sums, rows, second_rows)
    block(ns, early, first_stack, early_seconds, first_sums, old_second_sums, first_rows, early_second_rows)
    block(ns, ms, first_stack, second_stack, first_sums, second_sums, first_rows, second_rows)
    for group, (_, rows, _, old) in zip(groups, before):
        stats.append([[old[kind, n][:, 0:1] for n in range(len(group))] for kind in range(2)])
        blocks.append((group, early, rows, early_second_rows))
    copy.wait()
    message = base_ref[...]
    for k, (one, two, one_rows, two_rows) in enumerate(blocks):
        message = message + place(
            plan, one, two, *stats[k], one_rows, two_rows, index, picked_first.at[k], picked_second.at[k]
        )
    message_ref[...] = jnp.broadcast_to(message[None], message_ref.shape)


def power_kernel(plan, rays, gathered_ref, scores_ref, frames_ref, rows_ref, sorted_ref, matrix_ref):
    z, x, core, c = position()
    count, seconds = plan.count, plan.seconds
    for device in range(count):
        dz, rest = divmod(device, PAIR * PAIR * plan.cols)
        dx, rest = divmod(rest, PAIR * plan.cols)
        dk, dc = divmod(rest, plan.cols)
        rows_ref[pl.ds((dx * plan.cols + dc) * seconds + dz * PAIR + dk, 1), :] = gathered_ref[device]

    lane = lax.broadcasted_iota(jnp.int32, (seconds, plan.width), 1)
    block = (lane // seconds) % plan.firsts
    for to in range(plan.firsts):
        mixed = jnp.zeros((seconds, plan.width), jnp.float32)
        for b in range(plan.firsts):
            moved = rows_ref[b * seconds : (b + 1) * seconds, :]
            if b != to:
                moved = jnp.roll(moved, (b - to) * seconds, axis=1)
            mixed = jnp.where(block == b, moved, mixed)
        sorted_ref[to * seconds : (to + 1) * seconds, :] = mixed

    score = sorted_ref[:, :count]
    turn = 2.0 * math.pi / rays
    first = sorted_ref[:, count : 2 * count] * turn
    second = sorted_ref[:, 2 * count : 3 * count] * turn
    weighted = jnp.concatenate([score * jnp.cos(second), score * jnp.sin(second), score], axis=1)
    for p, unit in enumerate((jnp.cos(first), jnp.sin(first))):
        matrix_ref[p * count : (p + 1) * count, :] = weighted * jnp.concatenate([unit] * 3, axis=1)
    matrix_ref[2 * count :, :] = weighted

    begin = 3 * plan.pairs
    tile = begin // LANES * LANES
    turned = jnp.transpose(rows_ref[:, tile : tile + LANES])
    at = begin - tile
    frames = [
        jnp.concatenate([turned[at + 3 * k + q : at + 3 * k + q + 1] for q in range(3)], axis=1) for k in range(3)
    ]
    pad = jnp.zeros((5, 3 * count), jnp.float32)

    def applied(values):
        mixed = lax.dot_general(
            jnp.concatenate(values + [pad], axis=0),
            matrix_ref[...],
            (((1,), (1,)), ((), ())),
            precision=lax.Precision.HIGHEST,
            preferred_element_type=jnp.float32,
        )
        return [mixed[k : k + 1] for k in range(3)]

    def factor(y):
        g00, g10, g20, g11, g21, g22 = (
            jnp.sum(y[k] * y[l], axis=1, keepdims=True) for k, l in ((0, 0), (1, 0), (2, 0), (1, 1), (2, 1), (2, 2))
        )
        r0 = lax.rsqrt(g00)
        f10, f20 = g10 * r0, g20 * r0
        r1 = lax.rsqrt(g11 - f10 * f10)
        f21 = (g21 - f20 * f10) * r1
        r2 = lax.rsqrt(g22 - f20 * f20 - f21 * f21)
        return f10, f20, f21, r0, r1, r2

    def solved(parts, y):
        f10, f20, f21, r0, r1, r2 = parts
        v0 = y[0] * r0
        v1 = (y[1] - f10 * v0) * r1
        return [v0, v1, (y[2] - f20 * v0 - f21 * v1) * r2]

    y = applied(frames)
    for _ in range(ITERS - 1):
        y = solved(factor(y), applied(y))
    frames = solved(factor(y), y)

    own = (x * plan.cols + c) * seconds + z * PAIR + core
    wide = lax.broadcasted_iota(jnp.int32, (1, 3 * count), 1)
    three = lax.broadcasted_iota(jnp.int32, (1, 3), 1)
    for k in range(3):
        out = jnp.zeros((1, 3), jnp.float32)
        for q in range(3):
            value = jnp.sum(jnp.where(wide == q * count + own, frames[k], 0.0), axis=1, keepdims=True)
            out = jnp.where(three == q, value, out)
        frames_ref[k] = math.sqrt(count) * out

    source = lax.broadcasted_iota(jnp.int32, (seconds, plan.rows), 0)
    target = lax.broadcasted_iota(jnp.int32, (seconds, plan.rows), 1)
    lines = [jnp.zeros((1, plan.rows), jnp.float32) for _ in range(plan.cols)]
    for dx in range(PAIR):
        row = rows_ref[pl.ds((dx * plan.cols + c) * seconds + z * PAIR + core, 1), :]
        spread = (target == (source // PAIR) * (PAIR * PAIR) + dx * PAIR + source % PAIR).astype(jnp.float32)
        for dc in range(plan.cols):
            low = row[:, dc * seconds : (dc + 1) * seconds]
            high = row[:, (plan.cols + dc) * seconds : (plan.cols + dc + 1) * seconds]
            part = jnp.broadcast_to(jnp.where(x == 1, high, low), (8, seconds))
            moved = lax.dot_general(
                part,
                spread,
                (((1,), (0,)), ((), ())),
                precision=lax.Precision.HIGHEST,
                preferred_element_type=jnp.float32,
            )
            lines[dc] = lines[dc] + moved[0:1]
    for dc in range(plan.cols):
        scores_ref[dc] = lines[dc]


def scored(plan, polar_rays, first_line, second_line, start_frame):
    _, rays, depth = polar_rays.shape
    half = rays // 2
    half_tiled = -(-half // 8) * 8
    axes = ("row", "col")
    vmem = pl.BlockSpec(memory_space=pltpu.VMEM)

    def swap(value, distance):
        return lax.ppermute(value, axes, [(n, n ^ distance) for n in range(plan.count)])

    first = jnp.transpose(first_line, (0, 2, 1))
    second = jnp.transpose(second_line, (0, 2, 1))
    start = jnp.transpose(start_frame, (0, 2, 1))
    inputs = [pltpu.with_memory_space_constraint(one, pltpu.HBM) for one in (polar_rays, first, second, start)]
    own_rays, half_rays, own_frame = pl.pallas_call(
        functools.partial(prepare_kernel, plan),
        out_shape=(
            jax.ShapeDtypeStruct((1, rays + TABLE, depth), polar_rays.dtype),
            jax.ShapeDtypeStruct((1, half_tiled, depth), polar_rays.dtype),
            jax.ShapeDtypeStruct(start.shape, start.dtype),
        ),
        in_specs=[pl.BlockSpec(memory_space=pltpu.HBM)] * 4,
        out_specs=(vmem, vmem, vmem),
        scratch_shapes=[
            pltpu.VMEM(first.shape, first.dtype),
            pltpu.VMEM(second.shape, second.dtype),
            pltpu.SemaphoreType.DMA((7,)),
        ],
        compiler_params=pltpu.CompilerParams(vmem_limit_bytes=1 << 20),
        name="prepare",
    )(*inputs)
    fulls = [own_rays] + [swap(own_rays, plan.flat(0, n // plan.cols, 0, n % plan.cols)) for n in range(1, plan.firsts)]
    deep = [half_rays] + [swap(half_rays, plan.flat(dz, 0, 0, 0)) for dz in range(1, plan.depth)]
    halves = []
    for piece in deep:
        halves += [piece, swap(piece, plan.flat(0, 0, 1, 0))]

    first_height, second_height = -(-rays // 16) * 16, -(-half // 16) * 16
    params = pltpu.CompilerParams(vmem_limit_bytes=SCORE_VMEM)
    groups, late_ns = first_groups(plan)
    early_ms, late_ms = second_groups(plan)

    def first_shapes(ns):
        return [
            ((len(ns), first_height, depth), polar_rays.dtype),
            ((len(ns), rays, depth), jnp.float32),
            ((len(ns), depth), jnp.float32),
        ]

    def second_shapes(ms):
        return [
            ((len(ms), second_height, depth), polar_rays.dtype),
            ((len(ms), half, depth), jnp.float32),
            ((len(ms), depth), jnp.float32),
        ]

    most = max(len(early_ms), len(late_ms))
    span = max(len(ns) for ns in (*groups, late_ns)) * first_height
    before, seconds = [], None
    for ns in groups:
        shapes = first_shapes(ns) + [((2, len(ns), len(early_ms), LANES), jnp.float32)]
        inputs = [fulls[n] for n in ns]
        if seconds is None:
            shapes += second_shapes(early_ms)
            inputs += [halves[m] for m in early_ms]
        else:
            shapes += [((2, plan.index), jnp.int32), ((1, plan.width), jnp.float32)]
            inputs += [seconds[0], seconds[2], own_rays, own_frame]
        outs = pl.pallas_call(
            functools.partial(early_kernel, plan, rays, half, ns, early_ms, seconds is not None),
            out_shape=[jax.ShapeDtypeStruct(*one) for one in shapes],
            in_specs=[vmem] * len(inputs),
            out_specs=[vmem] * len(shapes),
            compiler_params=params,
            scratch_shapes=[pltpu.VMEM((most, span), jnp.float32)] * 2,
        )(*inputs)
        before += list(outs[:4])
        seconds = seconds or list(outs[4:])
    index, base = outs[4:]
    inputs = [fulls[n] for n in late_ns] + [halves[m] for m in late_ms] + before + seconds
    inputs += [index, base]
    kinds = 2 * len(groups) + 2
    message = pl.pallas_call(
        functools.partial(last_kernel, plan, rays, half, groups, early_ms, late_ns, late_ms),
        out_shape=jax.ShapeDtypeStruct((plan.count, 1, plan.width), jnp.float32),
        in_specs=[vmem] * len(inputs),
        out_specs=vmem,
        compiler_params=params,
        scratch_shapes=[
            pltpu.SMEM((2, plan.index), jnp.int32),
            pltpu.SemaphoreType.DMA,
        ]
        + [pltpu.VMEM(*one) for one in first_shapes(late_ns)[:2] + second_shapes(late_ms)[:2]]
        + [pltpu.VMEM((kinds, most, span), jnp.float32)] * 2
        + [pltpu.VMEM((kinds, most, depth), jnp.float32)] * 2,
        name="last",
    )(*inputs)

    gathered = lax.all_to_all(message, axes, 0, 0, tiled=True)

    scores, frames = pl.pallas_call(
        functools.partial(power_kernel, plan, rays),
        out_shape=(
            jax.ShapeDtypeStruct((plan.cols, 1, plan.rows), jnp.float32),
            jax.ShapeDtypeStruct((3, 1, 3), jnp.float32),
        ),
        in_specs=[vmem],
        out_specs=(vmem, vmem),
        compiler_params=pltpu.CompilerParams(vmem_limit_bytes=POWER_VMEM),
        scratch_shapes=[
            pltpu.VMEM((plan.count, plan.width), jnp.float32),
            pltpu.VMEM((plan.count, plan.width), jnp.float32),
            pltpu.VMEM((3 * plan.count, 3 * plan.count), jnp.float32),
        ],
        name="power",
    )(gathered)
    return jnp.transpose(scores, (0, 2, 1)), jnp.transpose(frames, (0, 2, 1))


def per_device(plan, *arrays):
    return scored(plan, *arrays)


def first_groups(plan):
    middle = range(plan.firsts - 2, 0, -1)
    cut = len(middle) // 2
    return ((0, plan.firsts - 1), tuple(middle[:cut])), tuple(middle[cut:])


def second_groups(plan):
    far = plan.depth - 1
    return tuple(range(PAIR * far)), tuple(range(PAIR * far, plan.seconds))


def solution(mesh):
    plan = Plan(mesh.shape["row"], mesh.shape["col"])
    placed = (
        P(("row", "col"), None, None),
        P("row", None, "col"),
        P("row", None, "col"),
        P(None, None, ("row", "col")),
    )
    return jax.shard_map(
        functools.partial(per_device, plan),
        mesh=mesh,
        in_specs=placed,
        out_specs=(P("row", None, "col"), P(None, None, ("row", "col"))),
        check_vma=False,
    )
```

```python
import functools
import math

import jax
import jax.numpy as jnp
from jax import lax
from jax.experimental import pallas as pl
from jax.experimental.pallas import tpu as pltpu
from jax.sharding import PartitionSpec as P

ITERS = 3
LANES = 128
TABLE = 8
CHUNK = 256
GROUP = 8
SCORE_VMEM = 24 << 20
POWER_VMEM = 16 << 20
PAIR = 2


class Plan:
    def __init__(self, rows, cols):
        self.rows, self.cols = rows, cols
        self.depth = rows // (PAIR * PAIR)
        self.count = rows * cols
        self.firsts = PAIR * cols
        self.seconds = PAIR * self.depth
        self.pairs = self.firsts * self.seconds
        self.width = -(-(3 * self.pairs + 9) // LANES) * LANES
        self.index = -(-self.pairs // LANES) * LANES

    def flat(self, z, x, core, c):
        return ((z * PAIR + x) * PAIR + core) * self.cols + c


def position():
    row, c = lax.axis_index("row"), lax.axis_index("col")
    return row // (PAIR * PAIR), (row // PAIR) % PAIR, row % PAIR, c


def prepare_kernel(
    plan, rays_ref, first_ref, second_ref, start_ref, full_ref, half_ref, frame_ref, first_row, second_row, sems
):
    rays, depth = rays_ref.shape[1:]
    half = half_ref.shape[1]
    cuts = [0, half // 16 * 8, half, half + (rays - half) // 16 * 8, rays]
    moves = [
        (rays_ref.at[:, pl.ds(low, high - low)], to.at[:, pl.ds(low, high - low)])
        for low, high, to in zip(cuts, cuts[1:], (half_ref, half_ref, full_ref, full_ref))
    ]
    moves += [(first_ref, first_row), (second_ref, second_row), (start_ref, frame_ref)]
    copies = [pltpu.make_async_copy(*move, sems.at[k]) for k, move in enumerate(moves)]
    for copy in copies:
        copy.start()
    for copy in copies:
        copy.wait()

    full_ref[0, :half] = half_ref[0]

    def row(table_ref):
        parts = [table_ref[c] for c in range(plan.cols)]
        spare = depth - plan.rows * plan.cols
        return jnp.concatenate(parts + [jnp.zeros((1, spare), jnp.int32)] * (spare > 0), axis=1)

    first, second = row(first_row), row(second_row)
    rows = jnp.concatenate([first >> 1, first & 1, second, jnp.zeros((TABLE - 3, depth), jnp.int32)], axis=0)
    full_ref[0, rays : rays + TABLE] = rows.astype(jnp.float32).astype(full_ref.dtype)


def pick_lines(own_table, next_table, own_at, next_at):
    chosen = 0.0
    for table, at in ((own_table, own_at), (next_table, next_at)):
        column = lax.broadcasted_iota(jnp.int32, (table.shape[1], at.shape[1]), 0)
        here = jnp.where(column == at, 1.0, 0.0).astype(table.dtype)
        chosen = chosen + jnp.dot(table, here, preferred_element_type=jnp.float32)
    return 2.0 * chosen[0:1] + chosen[1:2], chosen[2:3]


def lines(plan, own_table, next_table):
    z, x, core, c = position()
    number = lax.broadcasted_iota(jnp.int32, (1, plan.pairs), 1)
    dk, rest = number % PAIR, number // PAIR
    dz, rest = rest % plan.depth, rest // plan.depth
    dc, dx = rest % plan.cols, rest // plan.cols
    at = (c ^ dc) * plan.rows + ((z ^ dz) * PAIR + x) * PAIR + (core ^ dk)
    paired = pick_lines(own_table, next_table, jnp.where(dx == 0, at, -1), jnp.where(dx == 0, -1, at))
    at = dc * plan.rows + (dz * PAIR + x) * PAIR + dk
    sent = pick_lines(own_table, next_table, jnp.where(dx == x, at, -1), jnp.where(dx == x, -1, at))
    return paired, sent


def load_firsts(refs, stack, rows):
    sums = []
    for n, ref in enumerate(refs):
        stack[n, : ref.shape[1]] = ref[0]
        values = ref[0, : rows.shape[1]].astype(jnp.float32)
        rows[n] = values
        sums.append(jnp.sum(values, axis=0, keepdims=True))
    return sums


def load_seconds(refs, half, stack, rows):
    sums = []
    for m, ref in enumerate(refs):
        stack[m, : ref.shape[1]] = ref[0]
        values = ref[0, :half].astype(jnp.float32)
        rows[m] = values
        sums.append(jnp.sum(values, axis=0, keepdims=True))
    return sums


def cross(rays, half, firsts, seconds, first_sums, second_sums, means, parts):
    count, first_height, depth = firsts.shape
    second_count, second_height, _ = seconds.shape
    scale = 1.0 / (rays * half)
    second_sum = jnp.concatenate(second_sums, axis=0)
    centers = []
    for n in range(count):
        center = jnp.sum(second_sum * first_sums[n], axis=1, keepdims=True) * scale
        means[:second_count, n * first_height : (n + 1) * first_height] = jnp.broadcast_to(
            center, (second_count, first_height)
        )
        centers.append(center)
    total = count * first_height
    for begin in range(0, total, CHUNK):
        end = min(begin + CHUNK, total)
        wanted = firsts[...].reshape(total, depth)[begin:end]
        for low in range(0, second_count, GROUP):
            size = min(GROUP, second_count - low)
            corr = lax.dot_general(
                seconds[low : low + size].reshape(size * second_height, depth),
                wanted,
                (((1,), (1,)), ((), ())),
                preferred_element_type=jnp.float32,
            )
            for m in range(low, low + size):
                values = corr[(m - low) * second_height : (m - low) * second_height + half]
                top = jnp.maximum(values, means[m : m + 1, begin:end])
                parts[m : m + 1, begin:end] = jnp.sum(top, axis=0, keepdims=True)
    spreads = []
    for n in range(count):
        part = parts[:second_count, n * first_height : n * first_height + rays] - half * centers[n]
        spreads.append(jnp.sum(part, axis=1, keepdims=True) * (2.0 * scale))
    return centers, spreads


def place(plan, ns, ms, centers, spreads, first_rows, second_rows, index, picked_first, picked_second):
    z, x, core, c = position()
    slot = (((x * plan.cols + c) * plan.depth) + z) * PAIR + core
    wide = (len(ms), plan.width)
    row = lax.broadcasted_iota(jnp.int32, wide, 0)
    second = jnp.zeros(wide, jnp.int32)
    for m, name in enumerate(ms):
        second = jnp.where(row == m, name, second)
    lane = lax.broadcasted_iota(jnp.int32, wide, 1)
    placed = jnp.zeros(wide, jnp.float32)
    for n, name in enumerate(ns):
        for m in range(len(ms)):
            which = name * plan.seconds + ms[m]
            picked_first[m : m + 1, :] = first_rows[n, pl.ds(index[0, which], 1), :]
            picked_second[m : m + 1, :] = second_rows[m, pl.ds(index[1, which], 1), :]
        picked = jnp.sum(picked_first[: len(ms)] * picked_second[: len(ms)], axis=1, keepdims=True)
        score = (picked - centers[n]) / (spreads[n] + 1e-05)
        placed = placed + jnp.where(lane == slot ^ (name * plan.seconds + second), score, 0.0)
    return jnp.sum(placed, axis=0, keepdims=True)


def early_kernel(plan, rays, half, ns, ms, loaded, *refs):
    *refs, means, parts = refs
    firsts, refs = refs[: len(ns)], refs[len(ns) :]
    if loaded:
        second_stack, second_sum, *refs = refs
    else:
        seconds, refs = refs[: len(ms)], refs[len(ms) :]
    if plan.cols in ns:
        own_ref, start_ref, *refs = refs
    first_stack, first_rows, first_sum, stats, *refs = refs
    if loaded:
        second_sums = [second_sum[m : m + 1] for m in range(len(ms))]
    else:
        second_stack, second_rows, second_sum, *refs = refs
        second_sums = load_seconds(seconds, half, second_stack, second_rows)
        second_sum[...] = jnp.concatenate(second_sums, axis=0)
    if plan.cols in ns:
        index_ref, base_ref = refs
        tables = (ref[0, rays : rays + TABLE] for ref in (own_ref, firsts[ns.index(plan.cols)]))
        paired, sent = lines(plan, *tables)
        index_ref[0:1, : plan.pairs] = paired[0].astype(jnp.int32)
        index_ref[1:2, : plan.pairs] = paired[1].astype(jnp.int32)
        spare = plan.width - 3 * plan.pairs - 9
        base_ref[...] = jnp.concatenate(
            [jnp.zeros((1, plan.pairs), jnp.float32), *sent, *(start_ref[k] for k in range(3))]
            + [jnp.zeros((1, spare), jnp.float32)] * (spare > 0),
            axis=1,
        )
    first_sums = load_firsts(firsts, first_stack, first_rows)
    first_sum[...] = jnp.concatenate(first_sums, axis=0)
    centers, spreads = cross(rays, half, first_stack, second_stack, first_sums, second_sums, means, parts)
    for n in range(len(ns)):
        stats[0, n] = jnp.broadcast_to(centers[n], (len(ms), LANES))
        stats[1, n] = jnp.broadcast_to(spreads[n], (len(ms), LANES))


def last_kernel(plan, rays, half, groups, early, ns, ms, *refs):
    firsts, refs = refs[: len(ns)], refs[len(ns) :]
    seconds, refs = refs[: len(ms)], refs[len(ms) :]
    before, refs = [refs[4 * g : 4 * g + 4] for g in range(len(groups))], refs[4 * len(groups) :]
    early_seconds, early_second_rows, early_second_sum = refs[:3]
    index_ref, base_ref, message_ref, index, sem = refs[3:8]
    first_stack, first_rows, second_stack, second_rows, means, parts, picked_first, picked_second = refs[8:]
    copy = pltpu.make_async_copy(index_ref, index, sem)
    copy.start()
    second_sums = load_seconds(seconds, half, second_stack, second_rows)
    first_sums = load_firsts(firsts, first_stack, first_rows)
    old_second_sums = [early_second_sum[m : m + 1] for m in range(len(early))]

    blocks, stats = [], []

    def block(one, two, one_stack, two_stack, one_sums, two_sums, one_rows, two_rows):
        k = len(blocks)
        stats.append(cross(rays, half, one_stack, two_stack, one_sums, two_sums, means.at[k], parts.at[k]))
        blocks.append((one, two, one_rows, two_rows))

    for group, (stack, rows, sums, _) in zip(groups, before):
        old_sums = [sums[n : n + 1] for n in range(len(group))]
        block(group, ms, stack, second_stack, old_sums, second_sums, rows, second_rows)
    block(ns, early, first_stack, early_seconds, first_sums, old_second_sums, first_rows, early_second_rows)
    block(ns, ms, first_stack, second_stack, first_sums, second_sums, first_rows, second_rows)
    for group, (_, rows, _, old) in zip(groups, before):
        stats.append([[old[kind, n][:, 0:1] for n in range(len(group))] for kind in range(2)])
        blocks.append((group, early, rows, early_second_rows))
    copy.wait()
    message = base_ref[...]
    for k, (one, two, one_rows, two_rows) in enumerate(blocks):
        message = message + place(
            plan, one, two, *stats[k], one_rows, two_rows, index, picked_first.at[k], picked_second.at[k]
        )
    message_ref[...] = jnp.broadcast_to(message[None], message_ref.shape)


def power_kernel(plan, rays, gathered_ref, scores_ref, frames_ref, rows_ref, sorted_ref, matrix_ref):
    z, x, core, c = position()
    count, seconds = plan.count, plan.seconds
    for device in range(count):
        dz, rest = divmod(device, PAIR * PAIR * plan.cols)
        dx, rest = divmod(rest, PAIR * plan.cols)
        dk, dc = divmod(rest, plan.cols)
        rows_ref[pl.ds((dx * plan.cols + dc) * seconds + dz * PAIR + dk, 1), :] = gathered_ref[device]

    lane = lax.broadcasted_iota(jnp.int32, (seconds, plan.width), 1)
    block = (lane // seconds) % plan.firsts
    for to in range(plan.firsts):
        mixed = jnp.zeros((seconds, plan.width), jnp.float32)
        for b in range(plan.firsts):
            moved = rows_ref[b * seconds : (b + 1) * seconds, :]
            if b != to:
                moved = jnp.roll(moved, (b - to) * seconds, axis=1)
            mixed = jnp.where(block == b, moved, mixed)
        sorted_ref[to * seconds : (to + 1) * seconds, :] = mixed

    score = sorted_ref[:, :count]
    turn = 2.0 * math.pi / rays
    first = sorted_ref[:, count : 2 * count] * turn
    second = sorted_ref[:, 2 * count : 3 * count] * turn
    weighted = jnp.concatenate([score * jnp.cos(second), score * jnp.sin(second), score], axis=1)
    for p, unit in enumerate((jnp.cos(first), jnp.sin(first))):
        matrix_ref[p * count : (p + 1) * count, :] = weighted * jnp.concatenate([unit] * 3, axis=1)
    matrix_ref[2 * count :, :] = weighted

    begin = 3 * plan.pairs
    tile = begin // LANES * LANES
    turned = jnp.transpose(rows_ref[:, tile : tile + LANES])
    at = begin - tile
    frames = [
        jnp.concatenate([turned[at + 3 * k + q : at + 3 * k + q + 1] for q in range(3)], axis=1) for k in range(3)
    ]
    pad = jnp.zeros((5, 3 * count), jnp.float32)

    def applied(values):
        mixed = lax.dot_general(
            jnp.concatenate(values + [pad], axis=0),
            matrix_ref[...],
            (((1,), (1,)), ((), ())),
            precision=lax.Precision.HIGHEST,
            preferred_element_type=jnp.float32,
        )
        return [mixed[k : k + 1] for k in range(3)]

    def factor(y):
        g00, g10, g20, g11, g21, g22 = (
            jnp.sum(y[k] * y[l], axis=1, keepdims=True) for k, l in ((0, 0), (1, 0), (2, 0), (1, 1), (2, 1), (2, 2))
        )
        r0 = lax.rsqrt(g00)
        f10, f20 = g10 * r0, g20 * r0
        r1 = lax.rsqrt(g11 - f10 * f10)
        f21 = (g21 - f20 * f10) * r1
        r2 = lax.rsqrt(g22 - f20 * f20 - f21 * f21)
        return f10, f20, f21, r0, r1, r2

    def solved(parts, y):
        f10, f20, f21, r0, r1, r2 = parts
        v0 = y[0] * r0
        v1 = (y[1] - f10 * v0) * r1
        return [v0, v1, (y[2] - f20 * v0 - f21 * v1) * r2]

    y = applied(frames)
    for _ in range(ITERS - 1):
        y = solved(factor(y), applied(y))
    frames = solved(factor(y), y)

    own = (x * plan.cols + c) * seconds + z * PAIR + core
    wide = lax.broadcasted_iota(jnp.int32, (1, 3 * count), 1)
    three = lax.broadcasted_iota(jnp.int32, (1, 3), 1)
    for k in range(3):
        out = jnp.zeros((1, 3), jnp.float32)
        for q in range(3):
            value = jnp.sum(jnp.where(wide == q * count + own, frames[k], 0.0), axis=1, keepdims=True)
            out = jnp.where(three == q, value, out)
        frames_ref[k] = math.sqrt(count) * out

    source = lax.broadcasted_iota(jnp.int32, (seconds, plan.rows), 0)
    target = lax.broadcasted_iota(jnp.int32, (seconds, plan.rows), 1)
    lines = [jnp.zeros((1, plan.rows), jnp.float32) for _ in range(plan.cols)]
    for dx in range(PAIR):
        row = rows_ref[pl.ds((dx * plan.cols + c) * seconds + z * PAIR + core, 1), :]
        spread = (target == (source // PAIR) * (PAIR * PAIR) + dx * PAIR + source % PAIR).astype(jnp.float32)
        for dc in range(plan.cols):
            low = row[:, dc * seconds : (dc + 1) * seconds]
            high = row[:, (plan.cols + dc) * seconds : (plan.cols + dc + 1) * seconds]
            part = jnp.broadcast_to(jnp.where(x == 1, high, low), (8, seconds))
            moved = lax.dot_general(
                part,
                spread,
                (((1,), (0,)), ((), ())),
                precision=lax.Precision.HIGHEST,
                preferred_element_type=jnp.float32,
            )
            lines[dc] = lines[dc] + moved[0:1]
    for dc in range(plan.cols):
        scores_ref[dc] = lines[dc]


def scored(plan, polar_rays, first_line, second_line, start_frame):
    _, rays, depth = polar_rays.shape
    half = rays // 2
    half_tiled = -(-half // 8) * 8
    axes = ("row", "col")
    vmem = pl.BlockSpec(memory_space=pltpu.VMEM)

    def swap(value, distance):
        return lax.ppermute(value, axes, [(n, n ^ distance) for n in range(plan.count)])

    first = jnp.transpose(first_line, (0, 2, 1))
    second = jnp.transpose(second_line, (0, 2, 1))
    start = jnp.transpose(start_frame, (0, 2, 1))
    inputs = [pltpu.with_memory_space_constraint(one, pltpu.HBM) for one in (polar_rays, first, second, start)]
    own_rays, half_rays, own_frame = pl.pallas_call(
        functools.partial(prepare_kernel, plan),
        out_shape=(
            jax.ShapeDtypeStruct((1, rays + TABLE, depth), polar_rays.dtype),
            jax.ShapeDtypeStruct((1, half_tiled, depth), polar_rays.dtype),
            jax.ShapeDtypeStruct(start.shape, start.dtype),
        ),
        in_specs=[pl.BlockSpec(memory_space=pltpu.HBM)] * 4,
        out_specs=(vmem, vmem, vmem),
        scratch_shapes=[
            pltpu.VMEM(first.shape, first.dtype),
            pltpu.VMEM(second.shape, second.dtype),
            pltpu.SemaphoreType.DMA((7,)),
        ],
        compiler_params=pltpu.CompilerParams(vmem_limit_bytes=1 << 20),
        name="prepare",
    )(*inputs)
    fulls = [own_rays] + [swap(own_rays, plan.flat(0, n // plan.cols, 0, n % plan.cols)) for n in range(1, plan.firsts)]
    deep = [half_rays] + [swap(half_rays, plan.flat(dz, 0, 0, 0)) for dz in range(1, plan.depth)]
    halves = []
    for piece in deep:
        halves += [piece, swap(piece, plan.flat(0, 0, 1, 0))]

    first_height, second_height = -(-rays // 16) * 16, -(-half // 16) * 16
    params = pltpu.CompilerParams(vmem_limit_bytes=SCORE_VMEM)
    early_params = pltpu.CompilerParams(vmem_limit_bytes=SCORE_VMEM)
    groups, late_ns = first_groups(plan)
    early_ms, late_ms = second_groups(plan)

    def first_shapes(ns):
        return [
            ((len(ns), first_height, depth), polar_rays.dtype),
            ((len(ns), rays, depth), jnp.float32),
            ((len(ns), depth), jnp.float32),
        ]

    def second_shapes(ms):
        return [
            ((len(ms), second_height, depth), polar_rays.dtype),
            ((len(ms), half, depth), jnp.float32),
            ((len(ms), depth), jnp.float32),
        ]

    most = max(len(early_ms), len(late_ms))
    span = max(len(ns) for ns in (*groups, late_ns)) * first_height
    before, seconds = [], None
    for ns in groups:
        shapes = first_shapes(ns) + [((2, len(ns), len(early_ms), LANES), jnp.float32)]
        inputs = [fulls[n] for n in ns]
        inputs += [halves[m] for m in early_ms] if seconds is None else [seconds[0], seconds[2]]
        if seconds is None:
            shapes += second_shapes(early_ms)
        if plan.cols in ns:
            shapes += [((2, plan.index), jnp.int32), ((1, plan.width), jnp.float32)]
            inputs += [own_rays, own_frame]
        outs = pl.pallas_call(
            functools.partial(early_kernel, plan, rays, half, ns, early_ms, seconds is not None),
            out_shape=[jax.ShapeDtypeStruct(*one) for one in shapes],
            in_specs=[vmem] * len(inputs),
            out_specs=[vmem] * len(shapes),
            compiler_params=early_params,
            scratch_shapes=[pltpu.VMEM((most, span), jnp.float32)] * 2,
        )(*inputs)
        before += list(outs[:4])
        seconds = seconds or list(outs[4:7])
        if plan.cols in ns:
            index, base = outs[-2:]
    inputs = [fulls[n] for n in late_ns] + [halves[m] for m in late_ms] + before + seconds
    inputs += [index, base]
    kinds = 2 * len(groups) + 2
    message = pl.pallas_call(
        functools.partial(last_kernel, plan, rays, half, groups, early_ms, late_ns, late_ms),
        out_shape=jax.ShapeDtypeStruct((plan.count, 1, plan.width), jnp.float32),
        in_specs=[vmem] * len(inputs),
        out_specs=vmem,
        compiler_params=params,
        scratch_shapes=[
            pltpu.SMEM((2, plan.index), jnp.int32),
            pltpu.SemaphoreType.DMA,
        ]
        + [pltpu.VMEM(*one) for one in first_shapes(late_ns)[:2] + second_shapes(late_ms)[:2]]
        + [pltpu.VMEM((kinds, most, span), jnp.float32)] * 2
        + [pltpu.VMEM((kinds, most, depth), jnp.float32)] * 2,
        name="last",
    )(*inputs)

    gathered = lax.all_to_all(message, axes, 0, 0, tiled=True)

    scores, frames = pl.pallas_call(
        functools.partial(power_kernel, plan, rays),
        out_shape=(
            jax.ShapeDtypeStruct((plan.cols, 1, plan.rows), jnp.float32),
            jax.ShapeDtypeStruct((3, 1, 3), jnp.float32),
        ),
        in_specs=[vmem],
        out_specs=(vmem, vmem),
        compiler_params=pltpu.CompilerParams(vmem_limit_bytes=POWER_VMEM),
        scratch_shapes=[
            pltpu.VMEM((plan.count, plan.width), jnp.float32),
            pltpu.VMEM((plan.count, plan.width), jnp.float32),
            pltpu.VMEM((3 * plan.count, 3 * plan.count), jnp.float32),
        ],
        name="power",
    )(gathered)
    return jnp.transpose(scores, (0, 2, 1)), jnp.transpose(frames, (0, 2, 1))


def per_device(plan, *arrays):
    return scored(plan, *arrays)


def first_groups(plan):
    middle = range(plan.firsts - 2, 0, -1)
    cut = len(middle) // 2
    return ((0,), (plan.firsts - 1,), tuple(middle[:cut])), tuple(middle[cut:])


def second_groups(plan):
    far = plan.depth - 1
    return tuple(range(PAIR * far)), tuple(range(PAIR * far, plan.seconds))


def solution(mesh):
    plan = Plan(mesh.shape["row"], mesh.shape["col"])
    placed = (
        P(("row", "col"), None, None),
        P("row", None, "col"),
        P("row", None, "col"),
        P(None, None, ("row", "col")),
    )
    return jax.shard_map(
        functools.partial(per_device, plan),
        mesh=mesh,
        in_specs=placed,
        out_specs=(P("row", None, "col"), P(None, None, ("row", "col"))),
        check_vma=False,
    )
```
